128 devices in a mesh: slab: 16 (over x_lo, z, core), brick: 8 (over y, x_hi).
Axes of the slice: x: 4 (x_hi: 2, x_lo: 2; x = x_hi * 2 + x_lo), y: 4, z: 4, core: 2. Of those that a mesh axis runs over, the one named last changes fastest.
Arguments:
- features: bfloat16 [64, 262144], P(None, ('slab', 'brick')), may hold values from -6 to 6
- tangents: bfloat16 [4, 64, 262144], P(None, None, ('slab', 'brick')), may hold values from -6 to 6
- route: int32 [262144, 1], P(('slab', 'brick')), may hold values from 0 to 7; in each aligned block of 2048 rows (0 to 2047, 2048 to 4095, ...) at most 512 rows name the same one
- cell_local: int32 [262144], P(('slab', 'brick')), may hold values from 0 to 2047
- stencil: int32 [262144], P(('slab', 'brick')), may hold values from 0 to 7
- stencil_table: float32 [8, 64], replicated, may hold values from -6 to 6
- taps1: float32 [3, 3, 64], replicated, may hold values from -3.5 to 3.5
- taps2: float32 [3, 3, 64], replicated, may hold values from -3.5 to 3.5
- point1: bfloat16 [64, 64], replicated, may hold values from -0.75 to 0.75
- point2: bfloat16 [64, 64], replicated, may hold values from -0.75 to 0.75
- bias1: float32 [64], replicated, may hold values from -3 to 3
- bias2: float32 [64], replicated, may hold values from -3 to 3
- readout: float32 [64], replicated, may hold values from -12 to 12
Outputs:
- hvp: float32 [4, 64, 262144], P(None, None, ('slab', 'brick'))
The draws below stay inside these ranges and needn't reach their ends.
Inputs may be any that keep to these rules, and one draw needn't show every extreme that they name: `route`: at most 512 of the atoms of one device name one brick, and some device names some brick exactly 512 times.
All inputs are finite; a program needn't handle non-finite values.
Results may differ from the reference program's by a relative error of at most 0.008.
The reference program's roundings to bfloat16 on the way count: a program that leaves them out, or rounds other values in their place, can miss the bound.
Values may be sent and summed in bfloat16 or wider, within the bound.
A program may use at most 128 MiB of HBM per device.

```python
import math
import jax
import jax.numpy as jnp
import numpy as np
from jax import lax

NG = 64
CH = 64
NT = 4
KSETS = 8
ATOM_DEV = 2048
CAP = 512
CZ = 4
CY = 8
CELLS_DEV = 2048
ATOMS = 262144
N_BRICK = 8


def set_ends(entries, rng, low, top_value):
    extent = entries.shape
    index_at = [jax.random.randint(jax.random.fold_in(rng, axis), (), 0, extent[axis]) for axis in range(len(extent))]
    entries = entries.at[tuple(index_at)].set(low)
    longest = extent.index(max(extent))
    index_at[longest] = (index_at[longest] + 1) % extent[longest]
    return entries.at[tuple(index_at)].set(top_value)


def block_levels(own_key, extent, split, smallest, top_value):
    factor_of = 1.0
    for dim, shards_of in split:
        heights = jax.random.uniform(jax.random.fold_in(jax.random.fold_in(own_key, 6), dim), (shards_of,), jnp.float32, smallest / len(split), top_value / len(split))
        factor_of = factor_of * jnp.repeat(jnp.exp(heights), extent[dim] // shards_of).reshape((-1,) + (1,) * (len(extent) - 1 - dim))
    return factor_of


def deal_out(stream_key, own, number, rows, count, top, bound, skew):
    ranking = jax.random.permutation(stream_key, count)
    packed, usual = shares(count, rows * top, bound, skew, True), shares(count, rows * top, bound, skew, False)
    places = jnp.arange(count)

    def named(sizes, turn):
        used = int((sizes > 0).sum())
        fixed = max(1, used // 4)
        passed = fixed + (places - fixed + turn * (used - fixed)) % max(1, count - fixed)
        return jnp.zeros((count,), jnp.int32).at[ranking[jnp.where(places < fixed, places, passed)]].set(jnp.asarray(sizes, jnp.int32))

    sizes = jnp.where(number % 4 == 0, named(packed, number // 4), named(usual, number - number // 4 - 1))
    mixed = jax.random.permutation(jax.random.fold_in(own, 3), count)
    source_of, receiver = mixed[0:count // 2 * 2:2], mixed[1:count // 2 * 2:2]
    margin = jnp.minimum(sizes[source_of] - 1, bound - sizes[receiver]) // 2
    margin = jnp.where((source_of == ranking[0]) | (receiver == ranking[0]) | (sizes[receiver] == 0), 0, jnp.maximum(margin, 0))
    passed = jax.random.randint(jax.random.fold_in(own, 4), (count // 2,), 0, 1 << 20) % (margin + 1)
    sizes = sizes.at[source_of].add(-passed).at[receiver].add(passed)
    labels = jnp.searchsorted(jnp.cumsum(sizes), jnp.arange(rows * top), side="right").astype(jnp.int32)
    table = labels.reshape(top, rows).T
    table = table[jax.random.permutation(jax.random.fold_in(own, 1), rows)]
    turn = jax.random.randint(jax.random.fold_in(own, 2), (rows, 1), 0, top)
    return jnp.take_along_axis(table, (jnp.arange(top)[None, :] + turn) % top, axis=1)


def shares(amount, total, reach, skew, full):
    portions = [(1 << 20) // math.isqrt(grade ** skew) + 1 for grade in range(1, amount + 1)]
    largest = reach if full else min(reach, max(-(-total // amount), total * portions[0] // sum(portions)))
    least = 1 if total - largest >= amount - 1 else 0
    counts, rest = [largest] + [least] * (amount - 1), total - largest - least * (amount - 1)
    while rest > 0:
        movable = [i for i in range(1, amount) if counts[i] < largest] or [i for i in range(1, amount) if counts[i] < reach]
        pool, budget = sum([portions[i] for i in movable]), rest
        for i in movable:
            extra = min(reach - counts[i], max(1, budget * portions[i] // pool), rest)
            counts[i] = counts[i] + extra
            rest = rest - extra
    return np.array(counts)


def gaussian(own_key, dims, deviation, limit, split=(), kind=jnp.bfloat16):
    result = deviation * jax.random.normal(own_key, dims, jnp.float32)
    if split:
        result = result * block_levels(own_key, dims, split, -0.22, 0.18)
    return jnp.clip(result, -limit, limit).astype(kind)


def setup_inputs(seed: int = 0) -> dict:
    splits = jax.random.split(jax.random.key(seed), 14)
    features = gaussian(splits[0], (CH, ATOMS), 1.0, 6.0, ((1, 128),))
    tangents = gaussian(splits[1], (NT, CH, ATOMS), 1.0, 6.0, ((2, 128),))
    route_keys = jax.random.split(jax.random.fold_in(splits[2], 1), ATOMS // ATOM_DEV)
    route_turns = jax.random.permutation(jax.random.fold_in(splits[2], 3), ATOMS // ATOM_DEV)
    route = jax.vmap(lambda own, number: deal_out(jax.random.fold_in(splits[2], 2), own, number, ATOM_DEV, N_BRICK, 1, CAP, 2))(route_keys, route_turns).reshape((ATOMS, 1))
    cell_local = set_ends(jax.random.randint(splits[3], (ATOMS,), 0, CELLS_DEV), jax.random.fold_in(splits[3], 1), 0, CELLS_DEV - 1).astype(jnp.int32)
    stencil = set_ends(jax.random.randint(splits[4], (ATOMS,), 0, KSETS), jax.random.fold_in(splits[4], 1), 0, KSETS - 1).astype(jnp.int32)
    stencil_table = gaussian(splits[5], (KSETS, CH), 1.0, 6.0, (), jnp.float32)
    taps1 = gaussian(splits[6], (3, 3, CH), 0.6, 3.5, (), jnp.float32)
    taps2 = gaussian(splits[7], (3, 3, CH), 0.6, 3.5, (), jnp.float32)
    point1 = gaussian(splits[8], (CH, CH), CH ** -0.5, 0.75)
    point2 = gaussian(splits[9], (CH, CH), CH ** -0.5, 0.75)
    bias1 = gaussian(splits[10], (CH,), 0.5, 3.0, (), jnp.float32)
    bias2 = gaussian(splits[11], (CH,), 0.5, 3.0, (), jnp.float32)
    readout = gaussian(splits[12], (CH,), 2.0, 12.0, (), jnp.float32)
    return dict(features=features, tangents=tangents, route=route, cell_local=cell_local, stencil=stencil, stencil_table=stencil_table, taps1=taps1, taps2=taps2, point1=point1, point2=point2, bias1=bias1, bias2=bias2, readout=readout)


def dsilu(v):
    sg = jax.nn.sigmoid(v)
    return sg * (1.0 + v * (1.0 - sg))


def ddsilu(v):
    sg = jax.nn.sigmoid(v)
    return sg * (1.0 - sg) * (2.0 + v * (1.0 - 2.0 * sg))


def depth_ref(field, taps, flip):
    out = field.astype(jnp.float32)
    for axis in range(3):
        wts = taps[axis]
        if flip:
            wts = wts[::-1]
        lower = wts[0][:, None, None, None]
        middle = wts[1][:, None, None, None]
        upper = wts[2][:, None, None, None]
        out = lower * jnp.roll(out, 1, axis + 1) + middle * out + upper * jnp.roll(out, -1, axis + 1)
    return out


def mixing(point, field):
    return jnp.dot(point, field.reshape(CH, -1), preferred_element_type=jnp.float32).reshape(field.shape)


def reference(features, tangents, route, cell_local, stencil, stencil_table, taps1, taps2, point1, point2, bias1, bias2, readout):
    count_all = features.shape[1]
    index = jnp.arange(count_all, dtype=jnp.int32)
    slab_of = index // (N_BRICK * ATOM_DEV)
    brick_of = route[:, 0]
    z_part = cell_local // (CY * NG)
    y_part = (cell_local // NG) % CY
    x_part = cell_local % NG
    flat = ((slab_of * CZ + z_part) * NG + brick_of * CY + y_part) * NG + x_part
    tab = jnp.take(stencil_table, stencil, axis=0).T

    def deposit(values):
        dep = lax.optimization_barrier((values.astype(jnp.float32) * tab).astype(jnp.bfloat16))
        grid = jnp.zeros((CH, NG * NG * NG), jnp.float32).at[:, flat].add(dep.astype(jnp.float32))
        return grid.astype(jnp.bfloat16).reshape(CH, NG, NG, NG)

    bias_one = bias1[:, None, None, None]
    bias_two = bias2[:, None, None, None]
    scale = readout[:, None, None, None]
    charge = deposit(features)
    pre1 = mixing(point1, depth_ref(charge, taps1, False).astype(jnp.bfloat16)) + bias_one
    hidden = jax.nn.silu(pre1).astype(jnp.bfloat16)
    pre2 = mixing(point2, depth_ref(hidden, taps2, False).astype(jnp.bfloat16)) + bias_two
    g_two = (dsilu(pre2) * scale).astype(jnp.bfloat16)
    g_one = depth_ref(mixing(point2.T, g_two).astype(jnp.bfloat16), taps2, True)
    outputs = []
    for k in range(NT):
        tan_charge = deposit(tangents[k])
        t_one = mixing(point1, depth_ref(tan_charge, taps1, False).astype(jnp.bfloat16))
        moved = (dsilu(pre1) * t_one).astype(jnp.bfloat16)
        dz_two = mixing(point2, depth_ref(moved, taps2, False).astype(jnp.bfloat16))
        dg_two = (ddsilu(pre2) * scale * dz_two).astype(jnp.bfloat16)
        dg_one = depth_ref(mixing(point2.T, dg_two).astype(jnp.bfloat16), taps2, True)
        energy_term = (ddsilu(pre1) * t_one * g_one + dsilu(pre1) * dg_one).astype(jnp.bfloat16)
        back_one = mixing(point1.T, energy_term).astype(jnp.bfloat16)
        final = depth_ref(back_one, taps1, True).astype(jnp.bfloat16).reshape(CH, -1)
        outputs.append(jnp.take(final, flat, axis=1).astype(jnp.float32) * tab)
    return jnp.stack(outputs)
```

```python
import functools

import jax
import jax.numpy as jnp
from jax import lax
from jax.experimental import pallas as pl
from jax.experimental.pallas import tpu as pltpu
from jax.sharding import PartitionSpec as P

NG = 64
CH = 64
NT = 4
KSETS = 8
BRICKS = 8
SLABS = 16
ATOMS = 2048
CAP = 512
CZ = 4
CY = 8
XH = 32
LANES = 2 * CH
ROWS = CZ * CY * XH
HEAD = 16
GROUPS = ((0, HEAD + CH), (HEAD + CH, 2 * CH), (HEAD + 3 * CH, 2 * CH))
DEPTH = HEAD + (NT + 1) * CH
F32 = jnp.float32
BF16 = jnp.bfloat16
MESH = pl.DeviceIdType.MESH
VMEM = pl.BlockSpec(memory_space=pltpu.VMEM)


def table_rows(stencil_row, table_t):
    out = jnp.broadcast_to(table_t[:, 0:1], (CH, stencil_row.shape[1]))
    for k in range(1, KSETS):
        out = jnp.where(stencil_row == k, table_t[:, k : k + 1], out)
    return out


def pack_kernel(feat, tang, rel, cell, sten, table_t, out, slot_out, data, place, column):
    step = 512
    for c in range(ATOMS // step):
        cols = slice(c * step, (c + 1) * step)
        tab = table_rows(sten[:, cols], table_t[...])
        cells = cell[:, cols]
        high = (cells // NG + 1).astype(F32)
        low = (cells % NG).astype(F32)
        which = lax.broadcasted_iota(jnp.int32, (HEAD, step), 0)
        head = jnp.where(which == 0, high, jnp.where(which == 1, low, 0.0))
        data[0:HEAD, cols] = head.astype(BF16)
        data[HEAD : HEAD + CH, cols] = (feat[:, cols].astype(F32) * tab).astype(BF16)
        for k in range(NT):
            at = HEAD + (k + 1) * CH
            data[at : at + CH, cols] = (tang[k, :, cols].astype(F32) * tab).astype(BF16)
    width = 256
    upper = lax.broadcasted_iota(jnp.int32, (width, width), 0) <= lax.broadcasted_iota(
        jnp.int32, (width, width), 1
    )
    upper = jnp.where(upper, 1.0, 0.0).astype(BF16)
    carry = jnp.zeros((BRICKS, 1), F32)
    for c in range(ATOMS // width):
        cols = slice(c * width, (c + 1) * width)
        dest = rel[:, cols]
        hit = lax.broadcasted_iota(jnp.int32, (BRICKS, width), 0) == dest
        hot = jnp.where(hit, 1.0, 0.0)
        count = jnp.dot(hot.astype(BF16), upper, preferred_element_type=F32) + carry
        position = jnp.sum(jnp.where(hit, count, 0.0), axis=0, keepdims=True) - 1.0
        slot = dest.astype(F32) * CAP + position
        slot_out[:, cols] = slot.astype(jnp.int32)
        column[cols, :] = jnp.transpose(jnp.broadcast_to(slot, (8, width)))
        carry = carry + jnp.sum(hot, axis=1, keepdims=True)

    def one(r, _):
        base = (r * CAP).astype(F32)
        for c in range(ATOMS // 128):
            rows = slice(c * 128, (c + 1) * 128)
            lane = lax.broadcasted_iota(jnp.int32, (128, CAP), 1).astype(F32) + base
            place[rows, :] = jnp.where(column[rows, 0:1] == lane, 1.0, 0.0).astype(BF16)
        out[r] = jnp.dot(data[...], place[...], preferred_element_type=F32).astype(BF16)
        return 0

    lax.fori_loop(0, BRICKS, one, 0)


def unpack_kernel(back, slot, sten, table_t, out):
    width = slot.shape[1]
    acc = jnp.zeros((NT * CH, width), F32)
    for r in range(BRICKS):
        row = lax.broadcasted_iota(jnp.int32, (CAP, width), 0) + r * CAP
        place = jnp.where(row == slot[...], 1.0, 0.0).astype(BF16)
        acc = acc + jnp.dot(back[r], place, preferred_element_type=F32)
    tab = table_rows(sten[...], table_t[...])
    for k in range(NT):
        out[k] = acc[k * CH : (k + 1) * CH] * tab


def owner(brick):
    side = brick // 4
    return 2 * (brick + side * (7 - 2 * brick)) + side


def grid_kernel(
    packed, taps, w1, w1b, w2, w2b, rows3,
    back,
    recv, hot, ext, acc, t_one, slope, bend, curve, final, send,
    a_send, a_recv, h_send, h_recv, b_send, b_recv, own_sem,
):
    slab = lax.axis_index("slab")
    place = lax.axis_index("brick")
    x_hi = place % 2
    y = place // 2
    brick = y + x_hi * (7 - 2 * y)
    s_up, s_down = (slab + 1) % SLABS, (slab + SLABS - 1) % SLABS
    b_up, b_down = owner((brick + 1) % BRICKS), owner((brick + BRICKS - 1) % BRICKS)

    def at(s, b):
        return {"slab": s, "brick": b}

    peers = [at(slab, (place + r) % BRICKS) for r in range(1, BRICKS)]
    around = [
        at(s_down, place), at(s_up, place),
        at(s_down, b_down), at(s_down, b_up), at(s_up, b_down), at(s_up, b_up),
    ]
    gate = pltpu.get_barrier_semaphore()
    for peer in peers + around:
        pl.semaphore_signal(gate, inc=1, device_id=peer, device_id_type=MESH)
    pl.semaphore_wait(gate, len(peers) + len(around))

    def forward(g, r):
        start, size = GROUPS[g]
        return pltpu.make_async_remote_copy(
            src_ref=packed.at[r, pl.ds(start, size)],
            dst_ref=recv.at[r, pl.ds(start, size)],
            send_sem=a_send.at[g, r],
            recv_sem=a_recv.at[g, r],
            device_id=at(slab, (place + r) % BRICKS),
            device_id_type=MESH,
        )

    own = pltpu.make_async_copy(packed.at[0], recv.at[0], own_sem)
    own.start()
    for g in range(len(GROUPS)):
        for r in range(1, BRICKS):
            forward(g, r).start()
    own.wait()

    def halo(stage, v):
        e = stage * (NT + 1) + v
        field = ext.at[e]
        moves = (
            (field.at[1, pl.ds(1, CY)], field.at[CZ + 1, pl.ds(1, CY)], at(s_down, place)),
            (field.at[CZ, pl.ds(1, CY)], field.at[0, pl.ds(1, CY)], at(s_up, place)),
            (field.at[pl.ds(1, CZ), 1], field.at[pl.ds(1, CZ), CY + 1], at(slab, b_down)),
            (field.at[pl.ds(1, CZ), CY], field.at[pl.ds(1, CZ), 0], at(slab, b_up)),
            (field.at[1, 1], field.at[CZ + 1, CY + 1], at(s_down, b_down)),
            (field.at[1, CY], field.at[CZ + 1, 0], at(s_down, b_up)),
            (field.at[CZ, 1], field.at[0, CY + 1], at(s_up, b_down)),
            (field.at[CZ, CY], field.at[0, 0], at(s_up, b_up)),
        )
        return [
            pltpu.make_async_remote_copy(
                src_ref=src,
                dst_ref=dst,
                send_sem=h_send.at[e, i],
                recv_sem=h_recv.at[e, i],
                device_id=to,
                device_id_type=MESH,
            )
            for i, (src, dst, to) in enumerate(moves)
        ]

    def launch(stage, v):
        for copy in halo(stage, v):
            copy.start()

    def arrive(stage, v):
        for copy in halo(stage, v):
            copy.wait_recv()

    def split_mask(r):
        low = recv[r, 0:HEAD, :].astype(F32)[1:2, :]
        return low >= XH

    def make_hot(r):
        head = recv[r, 0:HEAD, :].astype(F32)
        high, low = head[0:1, :], head[1:2, :]
        label = (high - 1.0) * XH + jnp.where(low >= XH, low - XH, low)

        def block(i, _):
            row = (lax.broadcasted_iota(jnp.int32, (128, CAP), 0) + i * 128).astype(F32)
            hot[r, pl.ds(pl.multiple_of(i * 128, 128), 128), :] = jnp.where(
                row == label, 1.0, 0.0
            ).astype(BF16)
            return 0

        lax.fori_loop(0, ROWS // 128, block, 0)

    def deposit(g, first, vectors):
        width = LANES * vectors
        acc[:, 0:width] = jnp.zeros((ROWS, width), F32)

        def source(r, _):
            @pl.when(r > 0)
            def _():
                forward(g, r).wait_recv()

            if g == 0:
                make_hot(r)
            upper = split_mask(r)
            parts = []
            for i in range(vectors):
                rows = HEAD + (first + i) * CH
                value = recv[r, rows : rows + CH, :].astype(F32)
                parts.append(jnp.where(upper, 0.0, value).astype(BF16))
                parts.append(jnp.where(upper, value, 0.0).astype(BF16))
            spread = jnp.concatenate(parts, axis=0)
            acc[:, 0:width] += lax.dot_general(
                hot[r], spread, (((1,), (1,)), ((), ())), preferred_element_type=F32
            )
            return 0

        lax.fori_loop(0, BRICKS, source, 0)
        for i in range(vectors):
            for z in range(CZ):
                part = acc[z * CY * XH : (z + 1) * CY * XH, i * LANES : (i + 1) * LANES]
                ext[first + i, z + 1, 1 : CY + 1] = part.astype(BF16).reshape(CY, XH, LANES)
            launch(0, first + i)

    def convolve(stage, v, z):
        e = stage * (NT + 1) + v

        def weight(axis, tap):
            i = stage * 9 + axis * 3 + tap
            return taps[i : i + 1, :].reshape(1, 1, LANES)

        along = (
            weight(0, 0) * ext[e, z].astype(F32)
            + weight(0, 1) * ext[e, z + 1].astype(F32)
            + weight(0, 2) * ext[e, z + 2].astype(F32)
        )
        across = (
            weight(1, 0) * along[0:CY]
            + weight(1, 1) * along[1 : CY + 1]
            + weight(1, 2) * along[2 : CY + 2]
        )
        flat = across.reshape(CY, XH, LANES)
        sub = lax.broadcasted_iota(jnp.int32, (CY, 8, LANES), 1)
        back_one = pltpu.roll(flat, 1, 1)
        first = back_one[:, 0:8, :]
        first = jnp.where(sub == 0, pltpu.roll(first, CH, 2), first)
        before = jnp.concatenate([first, back_one[:, 8:, :]], axis=1)
        on_one = pltpu.roll(flat, XH - 1, 1)
        last = on_one[:, XH - 8 :, :]
        last = jnp.where(sub == 7, pltpu.roll(last, CH, 2), last)
        after = jnp.concatenate([on_one[:, : XH - 8, :], last], axis=1)
        out = weight(2, 0) * before + weight(2, 1) * flat + weight(2, 2) * after
        return out.reshape(CY * XH, LANES)

    plane = CY * XH

    def span(z):
        return pl.ds(pl.multiple_of(z * plane, plane), plane)

    def mix(value, weights):
        return jnp.dot(value.astype(BF16), weights[...], preferred_element_type=F32)

    def put(stage, v, z, value):
        ext[stage * (NT + 1) + v, z + 1, 1 : CY + 1] = value.astype(BF16).reshape(CY, XH, LANES)

    def planes(body):
        def step(z, _):
            body(z)
            return 0

        lax.fori_loop(0, CZ, step, 0)

    def sweep(stage, body, low, high):
        def step(v, _):
            arrive(stage, v)
            planes(functools.partial(body, v))
            if stage < 3:
                launch(stage + 1, v)
            return 0

        lax.fori_loop(low, high, step, 0)

    def base_one(v, z):
        pre = mix(convolve(0, 0, z), w1) + rows3[0:1, :]
        sg = jax.nn.sigmoid(pre)
        slope[span(z), :] = sg * (1.0 + pre * (1.0 - sg))
        bend[span(z), :] = sg * (1.0 - sg) * (2.0 + pre * (1.0 - 2.0 * sg))
        put(1, 0, z, pre * sg)

    def tangent_one(v, z):
        t = mix(convolve(0, v, z), w1)
        t_one[v - 1, span(z), :] = t
        put(1, v, z, slope[span(z), :] * t)

    def base_two(v, z):
        pre = mix(convolve(1, 0, z), w2) + rows3[1:2, :]
        sg = jax.nn.sigmoid(pre)
        scale = rows3[2:3, :]
        curve[span(z), :] = sg * (1.0 - sg) * (2.0 + pre * (1.0 - 2.0 * sg)) * scale
        put(2, 0, z, mix(sg * (1.0 + pre * (1.0 - sg)) * scale, w2b))

    def tangent_two(v, z):
        dz = mix(convolve(1, v, z), w2)
        put(2, v, z, mix(curve[span(z), :] * dz, w2b))

    def base_three(z):
        bend[span(z), :] = bend[span(z), :] * convolve(2, 0, z)

    def tangent_three(v, z):
        term = bend[span(z), :] * t_one[v - 1, span(z), :] + slope[span(z), :] * convolve(2, v, z)
        put(3, v, z, mix(term, w1b))

    def tangent_four(v, z):
        out = jnp.transpose(convolve(3, v, z)).astype(BF16)
        final[pl.ds(pl.multiple_of((v - 1) * LANES, LANES), LANES), span(z)] = out

    def backward(p, r):
        return pltpu.make_async_remote_copy(
            src_ref=send.at[r, pl.ds(p * LANES, LANES)],
            dst_ref=back.at[r, pl.ds(p * LANES, LANES)],
            send_sem=b_send.at[p, r],
            recv_sem=b_recv.at[p, r],
            device_id=at(slab, (place + BRICKS - r) % BRICKS),
            device_id_type=MESH,
        )

    def pick(p):
        def source(i, _):
            r = BRICKS - 1 - i
            got = jnp.dot(
                final[2 * p * LANES : 2 * (p + 1) * LANES, :], hot[r], preferred_element_type=F32
            )
            upper = split_mask(r)
            parts = []
            for k in range(2):
                at_k = k * LANES
                parts.append(
                    jnp.where(upper, got[at_k + CH : at_k + LANES], got[at_k : at_k + CH])
                )
            chosen = jnp.concatenate(parts, axis=0).astype(BF16)

            @pl.when(r > 0)
            def _():
                send[r, p * LANES : (p + 1) * LANES, :] = chosen
                backward(p, r).start()

            @pl.when(r == 0)
            def _():
                back[0, p * LANES : (p + 1) * LANES, :] = chosen

            return 0

        lax.fori_loop(0, BRICKS, source, 0)

    deposit(0, 0, 1)
    deposit(1, 1, 2)
    sweep(0, base_one, 0, 1)
    deposit(2, 3, 2)
    sweep(0, tangent_one, 1, 3)
    sweep(1, base_two, 0, 1)
    sweep(0, tangent_one, 3, 5)
    sweep(1, tangent_two, 1, 5)
    arrive(2, 0)
    planes(base_three)
    sweep(2, tangent_three, 1, 5)
    sweep(3, tangent_four, 1, 3)
    pick(0)
    sweep(3, tangent_four, 3, 5)
    pick(1)

    def finish(r, _):
        for p in range(2):
            backward(p, r).wait()
        for g in range(len(GROUPS)):
            forward(g, r).wait_send()
        return 0

    lax.fori_loop(1, BRICKS, finish, 0)

    def finish_halo(v, _):
        for stage in range(4):
            if stage == 3:
                @pl.when(v > 0)
                def _():
                    for copy in halo(3, v):
                        copy.wait_send()
            else:
                for copy in halo(stage, v):
                    copy.wait_send()
        return 0

    lax.fori_loop(0, NT + 1, finish_halo, 0)


def shards(
    features, tangents, route, cell_local, stencil, stencil_table,
    taps1, taps2, point1, point2, bias1, bias2, readout,
):
    table_t = stencil_table.T
    rel = (owner(route.reshape(1, ATOMS)) - lax.axis_index("brick") + BRICKS) % BRICKS
    cell = cell_local.reshape(1, ATOMS)
    sten = stencil.reshape(1, ATOMS)
    packed, slot = pl.pallas_call(
        pack_kernel,
        name="pack",
        out_shape=(
            jax.ShapeDtypeStruct((BRICKS, DEPTH, CAP), BF16),
            jax.ShapeDtypeStruct((1, ATOMS), jnp.int32),
        ),
        in_specs=[VMEM] * 6,
        out_specs=(VMEM, VMEM),
        scratch_shapes=[
            pltpu.VMEM((DEPTH, ATOMS), BF16),
            pltpu.VMEM((ATOMS, CAP), BF16),
            pltpu.VMEM((ATOMS, 8), F32),
        ],
    )(features, tangents, rel, cell, sten, table_t)

    def doubled(rows):
        return jnp.concatenate([rows, rows], axis=-1)

    forward_taps = [taps1.reshape(9, CH), taps2.reshape(9, CH)]
    flipped = [taps2[:, ::-1].reshape(9, CH), taps1[:, ::-1].reshape(9, CH)]
    taps = doubled(jnp.concatenate(forward_taps + flipped, axis=0))
    rows3 = doubled(jnp.stack([bias1, bias2, readout]))

    def block(w):
        zero = jnp.zeros_like(w)
        return jnp.concatenate(
            [jnp.concatenate([w, zero], axis=1), jnp.concatenate([zero, w], axis=1)], axis=0
        )

    fields = 4 * (NT + 1)
    dma = pltpu.SemaphoreType.DMA
    back = pl.pallas_call(
        grid_kernel,
        name="grid",
        out_shape=jax.ShapeDtypeStruct((BRICKS, NT * CH, CAP), BF16),
        in_specs=[VMEM] * 7,
        out_specs=VMEM,
        scratch_shapes=[
            pltpu.VMEM((BRICKS, DEPTH, CAP), BF16),
            pltpu.VMEM((BRICKS, ROWS, CAP), BF16),
            pltpu.VMEM((fields, CZ + 2, CY + 2, XH, LANES), BF16),
            pltpu.VMEM((ROWS, 2 * LANES), F32),
            pltpu.VMEM((NT, ROWS, LANES), F32),
            pltpu.VMEM((ROWS, LANES), F32),
            pltpu.VMEM((ROWS, LANES), F32),
            pltpu.VMEM((ROWS, LANES), F32),
            pltpu.VMEM((NT * LANES, ROWS), BF16),
            pltpu.VMEM((BRICKS, NT * CH, CAP), BF16),
            dma((3, BRICKS)),
            dma((3, BRICKS)),
            dma((fields, 8)),
            dma((fields, 8)),
            dma((2, BRICKS)),
            dma((2, BRICKS)),
            dma,
        ],
        compiler_params=pltpu.CompilerParams(
            collective_id=0, has_side_effects=True, vmem_limit_bytes=60 * 1024 * 1024
        ),
    )(packed, taps, block(point1.T), block(point1), block(point2.T), block(point2), rows3)
    width = 512
    return pl.pallas_call(
        unpack_kernel,
        name="unpack",
        grid=(ATOMS // width,),
        out_shape=jax.ShapeDtypeStruct((NT, CH, ATOMS), F32),
        in_specs=[
            pl.BlockSpec((BRICKS, NT * CH, CAP), lambda i: (0, 0, 0)),
            pl.BlockSpec((1, width), lambda i: (0, i)),
            pl.BlockSpec((1, width), lambda i: (0, i)),
            pl.BlockSpec((CH, KSETS), lambda i: (0, 0)),
        ],
        out_specs=pl.BlockSpec((NT, CH, width), lambda i: (0, 0, i)),
    )(back, slot, sten, table_t)


def solution(mesh):
    placed = (
        P(None, ("slab", "brick")),
        P(None, None, ("slab", "brick")),
        P(("slab", "brick"), None),
        P(("slab", "brick")),
        P(("slab", "brick")),
        P(),
        P(),
        P(),
        P(),
        P(),
        P(),
        P(),
        P(),
    )
    return jax.shard_map(
        shards,
        mesh=mesh,
        in_specs=placed,
        out_specs=P(None, None, ("slab", "brick")),
        check_vma=False,
    )
```

```python
import functools

import jax
import jax.numpy as jnp
from jax import lax
from jax.experimental import pallas as pl
from jax.experimental.pallas import tpu as pltpu
from jax.sharding import PartitionSpec as P

NG = 64
CH = 64
NT = 4
KSETS = 8
BRICKS = 8
SLABS = 16
ATOMS = 2048
CAP = 512
CZ = 4
CY = 8
XH = 32
LANES = 2 * CH
ROWS = CZ * CY * XH
HEAD = 16
GROUPS = ((0, HEAD + CH), (HEAD + CH, 2 * CH), (HEAD + 3 * CH, 2 * CH))
DEPTH = HEAD + (NT + 1) * CH
F32 = jnp.float32
BF16 = jnp.bfloat16
MESH = pl.DeviceIdType.MESH
VMEM = pl.BlockSpec(memory_space=pltpu.VMEM)


def owner(brick):
    side = brick // 4
    return 2 * (brick + side * (7 - 2 * brick)) + side


def twice(value):
    return jnp.concatenate([value, value], axis=-1)


def whole_kernel(
    feat, tang, route, cell, sten, table, taps_one, taps_two, point_one, point_two, bias_one, bias_two, readout,
    picked, tab,
    data, place_in, place_out, column, slots, packed, recv, hot, ext, acc, t_one, slope, bend, curve,
    final, send, got, total, taps, mixers, rows3,
    a_send, a_recv, h_send, h_recv, b_send, b_recv,
):
    slab = lax.axis_index("slab")
    place = lax.axis_index("brick")
    x_hi = place % 2
    y = place // 2
    brick = y + x_hi * (7 - 2 * y)
    s_up, s_down = (slab + 1) % SLABS, (slab + SLABS - 1) % SLABS
    b_up, b_down = owner((brick + 1) % BRICKS), owner((brick + BRICKS - 1) % BRICKS)

    def at(s, b):
        return {"slab": s, "brick": b}

    peers = [at(slab, (place + r) % BRICKS) for r in range(1, BRICKS)]
    around = [
        at(s_down, place), at(s_up, place),
        at(s_down, b_down), at(s_down, b_up), at(s_up, b_down), at(s_up, b_up),
    ]
    gate = pltpu.get_barrier_semaphore()
    for peer in peers + around:
        pl.semaphore_signal(gate, inc=1, device_id=peer, device_id_type=MESH)

    def forward(g, r):
        start, size = GROUPS[g]
        return pltpu.make_async_remote_copy(
            src_ref=packed.at[r, pl.ds(start, size)],
            dst_ref=recv.at[r, pl.ds(start, size)],
            send_sem=a_send.at[g, r],
            recv_sem=a_recv.at[g, r],
            device_id=at(slab, (place + r) % BRICKS),
            device_id_type=MESH,
        )

    def prepare():
        table_t = jnp.transpose(twice(table[...]))
        step = 512
        for c in range(ATOMS // step):
            cols = slice(c * step, (c + 1) * step)
            chosen = jnp.broadcast_to(table_t[0:CH, 0:1], (CH, step))
            for k in range(1, KSETS):
                chosen = jnp.where(sten[:, cols] == k, table_t[0:CH, k : k + 1], chosen)
            tab[:, cols] = chosen
            cells = cell[:, cols]
            high = (cells // NG + 1).astype(F32)
            low = (cells % NG).astype(F32)
            which = lax.broadcasted_iota(jnp.int32, (HEAD, step), 0)
            head = jnp.where(which == 0, high, jnp.where(which == 1, low, 0.0))
            data[0:HEAD, cols] = head.astype(BF16)
            data[HEAD : HEAD + CH, cols] = (feat[:, cols].astype(F32) * chosen).astype(BF16)
            for k in range(NT):
                start = HEAD + (k + 1) * CH
                data[start : start + CH, cols] = (tang[k, :, cols].astype(F32) * chosen).astype(BF16)
        width = 256
        upper = lax.broadcasted_iota(jnp.int32, (width, width), 0) <= lax.broadcasted_iota(
            jnp.int32, (width, width), 1
        )
        upper = jnp.where(upper, 1.0, 0.0).astype(BF16)
        carry = jnp.zeros((BRICKS, 1), F32)
        for c in range(ATOMS // width):
            cols = slice(c * width, (c + 1) * width)
            dest = (owner(route[:, cols]) - place + BRICKS) % BRICKS
            hit = lax.broadcasted_iota(jnp.int32, (BRICKS, width), 0) == dest
            one = jnp.where(hit, 1.0, 0.0)
            count = jnp.dot(one.astype(BF16), upper, preferred_element_type=F32) + carry
            position = jnp.sum(jnp.where(hit, count, 0.0), axis=0, keepdims=True) - 1.0
            slot = jnp.broadcast_to(dest.astype(F32) * CAP + position, (8, width))
            slots[:, cols] = slot
            column[cols, :] = jnp.transpose(slot)
            carry = carry + jnp.sum(one, axis=1, keepdims=True)
        for stage, (source, flip) in enumerate(
            ((taps_one, False), (taps_two, False), (taps_two, True), (taps_one, True))
        ):
            for axis in range(3):
                for tap in range(3):
                    i = stage * 9 + axis * 3 + tap
                    j = 2 - tap if flip else tap
                    taps[i : i + 1, :] = twice(source[axis, j : j + 1, :])
        rows3[0:1, :] = twice(bias_one[...])
        rows3[1:2, :] = twice(bias_two[...])
        rows3[2:3, :] = twice(readout[...])
        for i, point in enumerate((point_one, point_two)):
            value = point[...].astype(F32)
            zero = jnp.zeros_like(value)
            mixers[i, 0:CH, :] = jnp.concatenate([value, zero], axis=1).astype(BF16)
            mixers[i, CH:LANES, :] = jnp.concatenate([zero, value], axis=1).astype(BF16)

    def pack(r):
        base = r * CAP
        for c in range(ATOMS // 128):
            rows = slice(c * 128, (c + 1) * 128)
            lane = (lax.broadcasted_iota(jnp.int32, (128, CAP), 1) + base).astype(F32)
            place_in[rows, :] = jnp.where(column[rows, 0:1] == lane, 1.0, 0.0).astype(BF16)
        return jnp.dot(data[...], place_in[...], preferred_element_type=F32).astype(BF16)

    def unpack(p, r):
        def block(i, _):
            row = (lax.broadcasted_iota(jnp.int32, (64, ATOMS), 0) + (i * 64 + r * CAP)).astype(F32)
            place_out[pl.ds(pl.multiple_of(i * 64, 64), 64), :] = jnp.where(
                row == slots[0:1, :], 1.0, 0.0
            ).astype(BF16)
            return 0

        lax.fori_loop(0, CAP // 64, block, 0)
        rows = slice(p * LANES, (p + 1) * LANES)
        total[rows, :] += jnp.dot(got[r, rows, :], place_out[...], preferred_element_type=F32)

    def halo(stage, v):
        e = stage * (NT + 1) + v
        field = ext.at[e]
        moves = (
            (field.at[1, pl.ds(1, CY)], field.at[CZ + 1, pl.ds(1, CY)], at(s_down, place)),
            (field.at[CZ, pl.ds(1, CY)], field.at[0, pl.ds(1, CY)], at(s_up, place)),
            (field.at[pl.ds(1, CZ), 1], field.at[pl.ds(1, CZ), CY + 1], at(slab, b_down)),
            (field.at[pl.ds(1, CZ), CY], field.at[pl.ds(1, CZ), 0], at(slab, b_up)),
            (field.at[1, 1], field.at[CZ + 1, CY + 1], at(s_down, b_down)),
            (field.at[1, CY], field.at[CZ + 1, 0], at(s_down, b_up)),
            (field.at[CZ, 1], field.at[0, CY + 1], at(s_up, b_down)),
            (field.at[CZ, CY], field.at[0, 0], at(s_up, b_up)),
        )
        return [
            pltpu.make_async_remote_copy(
                src_ref=src,
                dst_ref=dst,
                send_sem=h_send.at[e, i],
                recv_sem=h_recv.at[e, i],
                device_id=to,
                device_id_type=MESH,
            )
            for i, (src, dst, to) in enumerate(moves)
        ]

    def launch(stage, v):
        for copy in halo(stage, v):
            copy.start()

    def arrive(stage, v):
        for copy in halo(stage, v):
            copy.wait_recv()

    def split_mask(r):
        low = recv[r, 0:HEAD, :].astype(F32)[1:2, :]
        return low >= XH

    def make_hot(r):
        head = recv[r, 0:HEAD, :].astype(F32)
        high, low = head[0:1, :], head[1:2, :]
        label = (high - 1.0) * XH + jnp.where(low >= XH, low - XH, low)

        def block(i, _):
            row = (lax.broadcasted_iota(jnp.int32, (128, CAP), 0) + i * 128).astype(F32)
            hot[r, pl.ds(pl.multiple_of(i * 128, 128), 128), :] = jnp.where(
                row == label, 1.0, 0.0
            ).astype(BF16)
            return 0

        lax.fori_loop(0, ROWS // 128, block, 0)

    def deposit(g, first, vectors):
        width = LANES * vectors
        acc[:, 0:width] = jnp.zeros((ROWS, width), F32)

        def source(r, _):
            @pl.when(r > 0)
            def _():
                forward(g, r).wait_recv()

            if g == 0:
                make_hot(r)
            upper = split_mask(r)
            parts = []
            for i in range(vectors):
                rows = HEAD + (first + i) * CH
                value = recv[r, rows : rows + CH, :].astype(F32)
                parts.append(jnp.where(upper, 0.0, value).astype(BF16))
                parts.append(jnp.where(upper, value, 0.0).astype(BF16))
            spread = jnp.concatenate(parts, axis=0)
            acc[:, 0:width] += lax.dot_general(
                hot[r], spread, (((1,), (1,)), ((), ())), preferred_element_type=F32
            )
            return 0

        lax.fori_loop(0, BRICKS, source, 0)
        for i in range(vectors):
            for z in range(CZ):
                part = acc[z * CY * XH : (z + 1) * CY * XH, i * LANES : (i + 1) * LANES]
                ext[first + i, z + 1, 1 : CY + 1] = part.astype(BF16).reshape(CY, XH, LANES)
            launch(0, first + i)

    def convolve(stage, v, z):
        e = stage * (NT + 1) + v

        def weight(axis, tap):
            i = stage * 9 + axis * 3 + tap
            return taps[i : i + 1, :].reshape(1, 1, LANES)

        along = (
            weight(0, 0) * ext[e, z].astype(F32)
            + weight(0, 1) * ext[e, z + 1].astype(F32)
            + weight(0, 2) * ext[e, z + 2].astype(F32)
        )
        across = (
            weight(1, 0) * along[0:CY]
            + weight(1, 1) * along[1 : CY + 1]
            + weight(1, 2) * along[2 : CY + 2]
        )
        flat = across.reshape(CY, XH, LANES)
        sub = lax.broadcasted_iota(jnp.int32, (CY, 8, LANES), 1)
        back_one = pltpu.roll(flat, 1, 1)
        first = back_one[:, 0:8, :]
        first = jnp.where(sub == 0, pltpu.roll(first, CH, 2), first)
        before = jnp.concatenate([first, back_one[:, 8:, :]], axis=1)
        on_one = pltpu.roll(flat, XH - 1, 1)
        last = on_one[:, XH - 8 :, :]
        last = jnp.where(sub == 7, pltpu.roll(last, CH, 2), last)
        after = jnp.concatenate([on_one[:, : XH - 8, :], last], axis=1)
        out = weight(2, 0) * before + weight(2, 1) * flat + weight(2, 2) * after
        return out.reshape(CY * XH, LANES)

    plane = CY * XH

    def span(z):
        return slice(z * plane, (z + 1) * plane)

    def mix(value, i, back):
        sides = ((1,), (0,)) if back else ((1,), (1,))
        return lax.dot_general(
            value.astype(BF16), mixers[i], (sides, ((), ())), preferred_element_type=F32
        )

    def put(stage, v, z, value):
        ext[stage * (NT + 1) + v, z + 1, 1 : CY + 1] = value.astype(BF16).reshape(CY, XH, LANES)

    def planes(body):
        for z in range(CZ):
            body(z)

    def sweep(stage, body, low, high):
        def step(v, _):
            arrive(stage, v)
            planes(functools.partial(body, v))
            if stage < 3:
                launch(stage + 1, v)
            return 0

        lax.fori_loop(low, high, step, 0)

    def base_one(v, z):
        pre = mix(convolve(0, 0, z), 0, False) + rows3[0:1, :]
        sg = jax.nn.sigmoid(pre)
        slope[span(z), :] = sg * (1.0 + pre * (1.0 - sg))
        bend[span(z), :] = sg * (1.0 - sg) * (2.0 + pre * (1.0 - 2.0 * sg))
        put(1, 0, z, pre * sg)

    def tangent_one(v, z):
        t = mix(convolve(0, v, z), 0, False)
        t_one[v - 1, span(z), :] = t
        put(1, v, z, slope[span(z), :] * t)

    def base_two(v, z):
        pre = mix(convolve(1, 0, z), 1, False) + rows3[1:2, :]
        sg = jax.nn.sigmoid(pre)
        scale = rows3[2:3, :]
        curve[span(z), :] = sg * (1.0 - sg) * (2.0 + pre * (1.0 - 2.0 * sg)) * scale
        put(2, 0, z, mix(sg * (1.0 + pre * (1.0 - sg)) * scale, 1, True))

    def tangent_two(v, z):
        dz = mix(convolve(1, v, z), 1, False)
        put(2, v, z, mix(curve[span(z), :] * dz, 1, True))

    def base_three(z):
        bend[span(z), :] = bend[span(z), :] * convolve(2, 0, z)

    def tangent_three(v, z):
        term = bend[span(z), :] * t_one[v - 1, span(z), :] + slope[span(z), :] * convolve(2, v, z)
        put(3, v, z, mix(term, 0, True))

    def tangent_four(v, z):
        out = jnp.transpose(convolve(3, v, z)).astype(BF16)
        final[pl.ds(pl.multiple_of((v - 1) * LANES, LANES), LANES), span(z)] = out

    def backward(p, r):
        return pltpu.make_async_remote_copy(
            src_ref=send.at[r, pl.ds(p * LANES, LANES)],
            dst_ref=got.at[r, pl.ds(p * LANES, LANES)],
            send_sem=b_send.at[p, r],
            recv_sem=b_recv.at[p, r],
            device_id=at(slab, (place + BRICKS - r) % BRICKS),
            device_id_type=MESH,
        )

    def pick(p):
        def source(i, _):
            r = BRICKS - 1 - i
            fetched = jnp.dot(
                final[2 * p * LANES : 2 * (p + 1) * LANES, :], hot[r], preferred_element_type=F32
            )
            upper = split_mask(r)
            parts = []
            for k in range(2):
                at_k = k * LANES
                parts.append(
                    jnp.where(upper, fetched[at_k + CH : at_k + LANES], fetched[at_k : at_k + CH])
                )
            chosen = jnp.concatenate(parts, axis=0).astype(BF16)

            @pl.when(r > 0)
            def _():
                send[r, p * LANES : (p + 1) * LANES, :] = chosen
                backward(p, r).start()

            @pl.when(r == 0)
            def _():
                got[0, p * LANES : (p + 1) * LANES, :] = chosen

            return 0

        lax.fori_loop(0, BRICKS, source, 0)

    prepare()
    recv[0] = pack(0)
    pl.semaphore_wait(gate, len(peers) + len(around))

    def pack_and_send(r, _):
        packed[r] = pack(r)
        forward(0, r).start()
        return 0

    lax.fori_loop(1, BRICKS, pack_and_send, 0)
    for g in range(1, len(GROUPS)):
        for r in range(1, BRICKS):
            forward(g, r).start()
    deposit(0, 0, 1)
    sweep(0, base_one, 0, 1)
    sweep(1, base_two, 0, 1)
    arrive(2, 0)
    planes(base_three)
    deposit(1, 1, 2)
    sweep(0, tangent_one, 1, 3)
    sweep(1, tangent_two, 1, 3)
    deposit(2, 3, 2)
    sweep(2, tangent_three, 1, 3)
    sweep(0, tangent_one, 3, 5)
    sweep(3, tangent_four, 1, 3)
    pick(0)
    sweep(1, tangent_two, 3, 5)
    sweep(2, tangent_three, 3, 5)
    sweep(3, tangent_four, 3, 5)
    pick(1)
    total[...] = jnp.zeros_like(total)
    for p in range(2):
        unpack(p, 0)

        def collect(r, _):
            backward(p, r).wait_recv()
            unpack(p, r)
            return 0

        lax.fori_loop(1, BRICKS, collect, 0)
    picked[...] = total[...].astype(BF16)

    def finish(r, _):
        for p in range(2):
            backward(p, r).wait_send()
        for g in range(len(GROUPS)):
            forward(g, r).wait_send()
        return 0

    lax.fori_loop(1, BRICKS, finish, 0)

    def finish_halo(v, _):
        for stage in range(4):
            if stage == 3:
                @pl.when(v > 0)
                def _():
                    for copy in halo(3, v):
                        copy.wait_send()
            else:
                for copy in halo(stage, v):
                    copy.wait_send()
        return 0

    lax.fori_loop(0, NT + 1, finish_halo, 0)


def shards(
    features, tangents, route, cell_local, stencil, stencil_table,
    taps1, taps2, point1, point2, bias1, bias2, readout,
):
    fields = 4 * (NT + 1)
    dma = pltpu.SemaphoreType.DMA
    picked, tab = pl.pallas_call(
        whole_kernel,
        name="whole",
        out_shape=(
            jax.ShapeDtypeStruct((NT * CH, ATOMS), BF16),
            jax.ShapeDtypeStruct((CH, ATOMS), F32),
        ),
        in_specs=[VMEM] * 13,
        out_specs=(VMEM, VMEM),
        scratch_shapes=[
            pltpu.VMEM((DEPTH, ATOMS), BF16),
            pltpu.VMEM((ATOMS, CAP), BF16),
            pltpu.VMEM((CAP, ATOMS), BF16),
            pltpu.VMEM((ATOMS, 8), F32),
            pltpu.VMEM((8, ATOMS), F32),
            pltpu.VMEM((BRICKS, DEPTH, CAP), BF16),
            pltpu.VMEM((BRICKS, DEPTH, CAP), BF16),
            pltpu.VMEM((BRICKS, ROWS, CAP), BF16),
            pltpu.VMEM((fields, CZ + 2, CY + 2, XH, LANES), BF16),
            pltpu.VMEM((ROWS, 2 * LANES), F32),
            pltpu.VMEM((NT, ROWS, LANES), F32),
            pltpu.VMEM((ROWS, LANES), F32),
            pltpu.VMEM((ROWS, LANES), F32),
            pltpu.VMEM((ROWS, LANES), F32),
            pltpu.VMEM((NT * LANES, ROWS), BF16),
            pltpu.VMEM((BRICKS, NT * CH, CAP), BF16),
            pltpu.VMEM((BRICKS, NT * CH, CAP), BF16),
            pltpu.VMEM((NT * CH, ATOMS), F32),
            pltpu.VMEM((40, LANES), F32),
            pltpu.VMEM((2, LANES, LANES), BF16),
            pltpu.VMEM((8, LANES), F32),
            dma((3, BRICKS)),
            dma((3, BRICKS)),
            dma((fields, 8)),
            dma((fields, 8)),
            dma((2, BRICKS)),
            dma((2, BRICKS)),
        ],
        compiler_params=pltpu.CompilerParams(
            collective_id=0, has_side_effects=True, vmem_limit_bytes=60 * 1024 * 1024
        ),
    )(
        features, tangents, route.reshape(1, ATOMS), cell_local.reshape(1, ATOMS), stencil.reshape(1, ATOMS),
        stencil_table, taps1, taps2, point1, point2,
        bias1.reshape(1, CH), bias2.reshape(1, CH), readout.reshape(1, CH),
    )
    return picked.reshape(NT, CH, ATOMS).astype(F32) * tab


def solution(mesh):
    placed = (
        P(None, ("slab", "brick")),
        P(None, None, ("slab", "brick")),
        P(("slab", "brick"), None),
        P(("slab", "brick")),
        P(("slab", "brick")),
        P(),
        P(),
        P(),
        P(),
        P(),
        P(),
        P(),
        P(),
    )
    return jax.shard_map(
        shards,
        mesh=mesh,
        in_specs=placed,
        out_specs=P(None, None, ("slab", "brick")),
        check_vma=False,
    )
```

```python
import functools

import jax
import jax.numpy as jnp
from jax import lax
from jax.experimental import pallas as pl
from jax.experimental.pallas import tpu as pltpu
from jax.sharding import PartitionSpec as P

NG = 64
CH = 64
NT = 4
KSETS = 8
BRICKS = 8
SLABS = 16
ATOMS = 2048
CAP = 512
CZ = 4
CY = 8
XH = 32
LANES = 2 * CH
ROWS = CZ * CY * XH
HEAD = 16
GROUPS = ((HEAD, 3 * CH), (HEAD + 3 * CH, 2 * CH), (0, HEAD))
DEPTH = HEAD + (NT + 1) * CH
F32 = jnp.float32
BF16 = jnp.bfloat16
MESH = pl.DeviceIdType.MESH
VMEM = pl.BlockSpec(memory_space=pltpu.VMEM)


def owner(brick):
    side = brick // 4
    return 2 * (brick + side * (7 - 2 * brick)) + side


def twice(value):
    return jnp.concatenate([value, value], axis=-1)


def whole_kernel(
    feat, tang, route, cell, sten, table, taps_one, taps_two, point_one, point_two, bias_one, bias_two, readout,
    picked, tab,
    data, place_in, place_out, column, slots, packed, recv, hot, ext, acc, t_one, slope, bend, curve,
    final, send, got, total, taps, mixers, rows3,
    a_send, a_recv, h_send, h_recv, b_send, b_recv,
):
    slab = lax.axis_index("slab")
    place = lax.axis_index("brick")
    x_hi = place % 2
    y = place // 2
    brick = y + x_hi * (7 - 2 * y)
    s_up, s_down = (slab + 1) % SLABS, (slab + SLABS - 1) % SLABS
    b_up, b_down = owner((brick + 1) % BRICKS), owner((brick + BRICKS - 1) % BRICKS)

    def at(s, b):
        return {"slab": s, "brick": b}

    peers = [at(slab, (place + r) % BRICKS) for r in range(1, BRICKS)]
    around = [
        at(s_down, place), at(s_up, place),
        at(s_down, b_down), at(s_down, b_up), at(s_up, b_down), at(s_up, b_up),
    ]
    gate = pltpu.get_barrier_semaphore()
    for peer in peers + around:
        pl.semaphore_signal(gate, inc=1, device_id=peer, device_id_type=MESH)

    def forward(g, r):
        start, size = GROUPS[g]
        return pltpu.make_async_remote_copy(
            src_ref=packed.at[r, pl.ds(start, size)],
            dst_ref=recv.at[r, pl.ds(start, size)],
            send_sem=a_send.at[g, r],
            recv_sem=a_recv.at[g, r],
            device_id=at(slab, (place + r) % BRICKS),
            device_id_type=MESH,
        )

    def prepare():
        table_t = jnp.transpose(twice(table[...]))
        step = 512
        for c in range(ATOMS // step):
            cols = slice(c * step, (c + 1) * step)
            chosen = jnp.broadcast_to(table_t[0:CH, 0:1], (CH, step))
            for k in range(1, KSETS):
                chosen = jnp.where(sten[:, cols] == k, table_t[0:CH, k : k + 1], chosen)
            tab[:, cols] = chosen
            cells = cell[:, cols]
            high = (cells // NG + 1).astype(F32)
            low = (cells % NG).astype(F32)
            which = lax.broadcasted_iota(jnp.int32, (HEAD, step), 0)
            head = jnp.where(which == 0, high, jnp.where(which == 1, low, 0.0))
            data[0:HEAD, cols] = head.astype(BF16)
            data[HEAD : HEAD + CH, cols] = (feat[:, cols].astype(F32) * chosen).astype(BF16)
            for k in range(NT):
                start = HEAD + (k + 1) * CH
                data[start : start + CH, cols] = (tang[k, :, cols].astype(F32) * chosen).astype(BF16)
        width = 256
        upper = lax.broadcasted_iota(jnp.int32, (width, width), 0) <= lax.broadcasted_iota(
            jnp.int32, (width, width), 1
        )
        upper = jnp.where(upper, 1.0, 0.0).astype(BF16)
        carry = jnp.zeros((BRICKS, 1), F32)
        for c in range(ATOMS // width):
            cols = slice(c * width, (c + 1) * width)
            dest = (owner(route[:, cols]) - place + BRICKS) % BRICKS
            hit = lax.broadcasted_iota(jnp.int32, (BRICKS, width), 0) == dest
            one = jnp.where(hit, 1.0, 0.0)
            count = jnp.dot(one.astype(BF16), upper, preferred_element_type=F32) + carry
            position = jnp.sum(jnp.where(hit, count, 0.0), axis=0, keepdims=True) - 1.0
            slot = jnp.broadcast_to(dest.astype(F32) * CAP + position, (8, width))
            slots[:, cols] = slot
            column[cols, :] = jnp.transpose(slot)
            carry = carry + jnp.sum(one, axis=1, keepdims=True)
        for stage, (source, flip) in enumerate(
            ((taps_one, False), (taps_two, False), (taps_two, True), (taps_one, True))
        ):
            for axis in range(3):
                for tap in range(3):
                    i = stage * 9 + axis * 3 + tap
                    j = 2 - tap if flip else tap
                    taps[i : i + 1, :] = twice(source[axis, j : j + 1, :])
        rows3[0:1, :] = twice(bias_one[...])
        rows3[1:2, :] = twice(bias_two[...])
        rows3[2:3, :] = twice(readout[...])
        for i, point in enumerate((point_one, point_two)):
            value = point[...].astype(F32)
            zero = jnp.zeros_like(value)
            mixers[i, 0:CH, :] = jnp.concatenate([value, zero], axis=1).astype(BF16)
            mixers[i, CH:LANES, :] = jnp.concatenate([zero, value], axis=1).astype(BF16)

    def pack(r):
        base = r * CAP
        for c in range(ATOMS // 128):
            rows = slice(c * 128, (c + 1) * 128)
            lane = (lax.broadcasted_iota(jnp.int32, (128, CAP), 1) + base).astype(F32)
            place_in[rows, :] = jnp.where(column[rows, 0:1] == lane, 1.0, 0.0).astype(BF16)
        return jnp.dot(data[...], place_in[...], preferred_element_type=F32).astype(BF16)

    def unpack(r):
        def block(i, _):
            row = (lax.broadcasted_iota(jnp.int32, (64, ATOMS), 0) + (i * 64 + r * CAP)).astype(F32)
            place_out[pl.ds(pl.multiple_of(i * 64, 64), 64), :] = jnp.where(
                row == slots[0:1, :], 1.0, 0.0
            ).astype(BF16)
            return 0

        lax.fori_loop(0, CAP // 64, block, 0)
        return jnp.dot(got[r], place_out[...], preferred_element_type=F32)

    def halo(stage, v):
        e = stage * (NT + 1) + v
        field = ext.at[e]
        moves = (
            (field.at[1, 1], field.at[CZ + 1, CY + 1], at(s_down, b_down)),
            (field.at[1, CY], field.at[CZ + 1, 0], at(s_down, b_up)),
            (field.at[CZ, 1], field.at[0, CY + 1], at(s_up, b_down)),
            (field.at[CZ, CY], field.at[0, 0], at(s_up, b_up)),
            (field.at[pl.ds(1, CZ), 1], field.at[pl.ds(1, CZ), CY + 1], at(slab, b_down)),
            (field.at[pl.ds(1, CZ), CY], field.at[pl.ds(1, CZ), 0], at(slab, b_up)),
            (field.at[1, pl.ds(1, CY)], field.at[CZ + 1, pl.ds(1, CY)], at(s_down, place)),
            (field.at[CZ, pl.ds(1, CY)], field.at[0, pl.ds(1, CY)], at(s_up, place)),
        )
        return [
            pltpu.make_async_remote_copy(
                src_ref=src,
                dst_ref=dst,
                send_sem=h_send.at[e, i],
                recv_sem=h_recv.at[e, i],
                device_id=to,
                device_id_type=MESH,
            )
            for i, (src, dst, to) in enumerate(moves)
        ]

    def launch(stage, v):
        for copy in halo(stage, v):
            copy.start()

    def arrive(stage, v):
        for copy in halo(stage, v):
            copy.wait_recv()

    def split_mask(r):
        low = recv[r, 0:HEAD, :].astype(F32)[1:2, :]
        return low >= XH

    def make_hot(r):
        head = recv[r, 0:HEAD, :].astype(F32)
        high, low = head[0:1, :], head[1:2, :]
        label = (high - 1.0) * XH + jnp.where(low >= XH, low - XH, low)

        def block(i, _):
            row = (lax.broadcasted_iota(jnp.int32, (128, CAP), 0) + i * 128).astype(F32)
            hot[r, pl.ds(pl.multiple_of(i * 128, 128), 128), :] = jnp.where(
                row == label, 1.0, 0.0
            ).astype(BF16)
            return 0

        lax.fori_loop(0, ROWS // 128, block, 0)

    def deposit(g, low, high):
        vectors, first = (3, 0) if g == 0 else (2, 3)
        width = LANES * vectors

        def source(r, _):
            if low > 0:
                forward(g, r).wait_recv()
            upper = split_mask(r)
            parts = []
            for i in range(vectors):
                rows = HEAD + (first + i) * CH
                value = recv[r, rows : rows + CH, :].astype(F32)
                parts.append(jnp.where(upper, 0.0, value).astype(BF16))
                parts.append(jnp.where(upper, value, 0.0).astype(BF16))
            spread = jnp.concatenate(parts, axis=0)
            more = lax.dot_general(
                hot[r], spread, (((1,), (1,)), ((), ())), preferred_element_type=F32
            )
            if low > 0:
                acc[:, 0:width] += more
            else:
                acc[:, 0:width] = more
            return 0

        if low == 0:
            source(0, 0)
        else:
            lax.fori_loop(low, high, source, 0)
        if high == BRICKS:
            for i in range(vectors):
                for z in range(CZ):
                    part = acc[z * CY * XH : (z + 1) * CY * XH, i * LANES : (i + 1) * LANES]
                    ext[first + i, z + 1, 1 : CY + 1] = part.astype(BF16).reshape(CY, XH, LANES)
                launch(0, first + i)

    def bulk(g, low, high):
        for r in range(low, high):
            forward(g, r).start()

    def convolve(stage, v, z):
        e = stage * (NT + 1) + v

        def weight(axis, tap):
            i = stage * 9 + axis * 3 + tap
            return taps[i : i + 1, :].reshape(1, 1, LANES)

        along = (
            weight(0, 0) * ext[e, z].astype(F32)
            + weight(0, 1) * ext[e, z + 1].astype(F32)
            + weight(0, 2) * ext[e, z + 2].astype(F32)
        )
        across = (
            weight(1, 0) * along[0:CY]
            + weight(1, 1) * along[1 : CY + 1]
            + weight(1, 2) * along[2 : CY + 2]
        )
        flat = across.reshape(CY, XH, LANES)
        sub = lax.broadcasted_iota(jnp.int32, (CY, 8, LANES), 1)
        back_one = pltpu.roll(flat, 1, 1)
        first = back_one[:, 0:8, :]
        first = jnp.where(sub == 0, pltpu.roll(first, CH, 2), first)
        before = jnp.concatenate([first, back_one[:, 8:, :]], axis=1)
        on_one = pltpu.roll(flat, XH - 1, 1)
        last = on_one[:, XH - 8 :, :]
        last = jnp.where(sub == 7, pltpu.roll(last, CH, 2), last)
        after = jnp.concatenate([on_one[:, : XH - 8, :], last], axis=1)
        out = weight(2, 0) * before + weight(2, 1) * flat + weight(2, 2) * after
        return out.reshape(CY * XH, LANES)

    plane = CY * XH

    def span(z):
        return slice(z * plane, (z + 1) * plane)

    def mix(value, i, back):
        sides = ((1,), (0,)) if back else ((1,), (1,))
        return lax.dot_general(
            value.astype(BF16), mixers[i], (sides, ((), ())), preferred_element_type=F32
        )

    def put(stage, v, z, value):
        ext[stage * (NT + 1) + v, z + 1, 1 : CY + 1] = value.astype(BF16).reshape(CY, XH, LANES)

    def planes(body):
        for z in range(CZ):
            body(z)

    def sweep(stage, body, low, high):
        def step(v, _):
            arrive(stage, v)
            planes(functools.partial(body, v))
            if stage < 3:
                launch(stage + 1, v)
            return 0

        lax.fori_loop(low, high, step, 0)

    def base_one(v, z):
        pre = mix(convolve(0, 0, z), 0, False) + rows3[0:1, :]
        sg = jax.nn.sigmoid(pre)
        slope[span(z), :] = sg * (1.0 + pre * (1.0 - sg))
        bend[span(z), :] = sg * (1.0 - sg) * (2.0 + pre * (1.0 - 2.0 * sg))
        put(1, 0, z, pre * sg)

    def tangent_one(v, z):
        t = mix(convolve(0, v, z), 0, False)
        t_one[v - 1, span(z), :] = t
        put(1, v, z, slope[span(z), :] * t)

    def base_two(v, z):
        pre = mix(convolve(1, 0, z), 1, False) + rows3[1:2, :]
        sg = jax.nn.sigmoid(pre)
        scale = rows3[2:3, :]
        curve[span(z), :] = sg * (1.0 - sg) * (2.0 + pre * (1.0 - 2.0 * sg)) * scale
        put(2, 0, z, mix(sg * (1.0 + pre * (1.0 - sg)) * scale, 1, True))

    def tangent_two(v, z):
        dz = mix(convolve(1, v, z), 1, False)
        put(2, v, z, mix(curve[span(z), :] * dz, 1, True))

    def base_three(z):
        bend[span(z), :] = bend[span(z), :] * convolve(2, 0, z)

    def tangent_three(v, z):
        term = bend[span(z), :] * t_one[v - 1, span(z), :] + slope[span(z), :] * convolve(2, v, z)
        put(3, v, z, mix(term, 0, True))

    def tangent_four(v, z):
        out = jnp.transpose(convolve(3, v, z)).astype(BF16)
        final[pl.ds(pl.multiple_of((v - 1) * LANES, LANES), LANES), span(z)] = out

    def backward(p, r):
        return pltpu.make_async_remote_copy(
            src_ref=send.at[r, pl.ds(p * LANES, LANES)],
            dst_ref=got.at[r, pl.ds(p * LANES, LANES)],
            send_sem=b_send.at[p, r],
            recv_sem=b_recv.at[p, r],
            device_id=at(slab, (place + BRICKS - r) % BRICKS),
            device_id_type=MESH,
        )

    def pick(p, low, high):
        def source(r, _):
            fetched = jnp.dot(
                final[2 * p * LANES : 2 * (p + 1) * LANES, :], hot[r], preferred_element_type=F32
            )
            upper = split_mask(r)
            parts = []
            for k in range(2):
                at_k = k * LANES
                parts.append(
                    jnp.where(upper, fetched[at_k + CH : at_k + LANES], fetched[at_k : at_k + CH])
                )
            chosen = jnp.concatenate(parts, axis=0).astype(BF16)

            @pl.when(r > 0)
            def _():
                send[r, p * LANES : (p + 1) * LANES, :] = chosen
                backward(p, r).start()

            @pl.when(r == 0)
            def _():
                got[0, p * LANES : (p + 1) * LANES, :] = chosen

            return 0

        lax.fori_loop(low, high, source, 0)

    def collect(r, _):
        for p in range(2):
            backward(p, r).wait_recv()
        total[...] += unpack(r)
        return 0

    prepare()
    recv[0] = pack(0)

    def pack_only(r, _):
        packed[r] = pack(r)
        return 0

    def pack_and_send(r, _):
        packed[r] = pack(r)
        forward(2, r).start()
        forward(0, r).start()
        return 0

    early = 4
    lax.fori_loop(1, early, pack_only, 0)
    pl.semaphore_wait(gate, len(peers) + len(around))
    for r in range(1, early):
        forward(2, r).start()
        forward(0, r).start()
    lax.fori_loop(early, BRICKS, pack_and_send, 0)
    bulk(1, 1, BRICKS)
    make_hot(0)
    deposit(0, 0, 1)

    def mark(r, _):
        forward(2, r).wait_recv()
        make_hot(r)
        return 0

    lax.fori_loop(1, BRICKS, mark, 0)
    deposit(0, 1, 8)
    sweep(0, base_one, 0, 1)
    sweep(0, tangent_one, 1, 3)
    deposit(1, 0, 1)
    deposit(1, 1, 8)
    sweep(1, base_two, 0, 1)
    sweep(1, tangent_two, 1, 3)
    sweep(0, tangent_one, 3, 5)
    arrive(2, 0)
    planes(base_three)
    sweep(2, tangent_three, 1, 3)
    sweep(1, tangent_two, 3, 5)
    sweep(3, tangent_four, 1, 3)
    pick(0, 0, 2)
    sweep(2, tangent_three, 3, 5)
    pick(0, 2, 8)
    sweep(3, tangent_four, 3, 5)
    pick(1, 0, 8)
    total[...] = unpack(0)
    lax.fori_loop(1, BRICKS, collect, 0)
    picked[...] = total[...].astype(BF16)

    def finish(r, _):
        for p in range(2):
            backward(p, r).wait_send()
        for g in range(len(GROUPS)):
            forward(g, r).wait_send()
        return 0

    lax.fori_loop(1, BRICKS, finish, 0)

    def finish_halo(v, _):
        for stage in range(4):
            if stage == 3:
                @pl.when(v > 0)
                def _():
                    for copy in halo(3, v):
                        copy.wait_send()
            else:
                for copy in halo(stage, v):
                    copy.wait_send()
        return 0

    lax.fori_loop(0, NT + 1, finish_halo, 0)


def shards(
    features, tangents, route, cell_local, stencil, stencil_table,
    taps1, taps2, point1, point2, bias1, bias2, readout,
):
    fields = 4 * (NT + 1)
    dma = pltpu.SemaphoreType.DMA
    picked, tab = pl.pallas_call(
        whole_kernel,
        name="whole",
        out_shape=(
            jax.ShapeDtypeStruct((NT * CH, ATOMS), BF16),
            jax.ShapeDtypeStruct((CH, ATOMS), F32),
        ),
        in_specs=[VMEM] * 13,
        out_specs=(VMEM, VMEM),
        scratch_shapes=[
            pltpu.VMEM((DEPTH, ATOMS), BF16),
            pltpu.VMEM((ATOMS, CAP), BF16),
            pltpu.VMEM((CAP, ATOMS), BF16),
            pltpu.VMEM((ATOMS, 8), F32),
            pltpu.VMEM((8, ATOMS), F32),
            pltpu.VMEM((BRICKS, DEPTH, CAP), BF16),
            pltpu.VMEM((BRICKS, DEPTH, CAP), BF16),
            pltpu.VMEM((BRICKS, ROWS, CAP), BF16),
            pltpu.VMEM((fields, CZ + 2, CY + 2, XH, LANES), BF16),
            pltpu.VMEM((ROWS, 3 * LANES), F32),
            pltpu.VMEM((NT, ROWS, LANES), F32),
            pltpu.VMEM((ROWS, LANES), F32),
            pltpu.VMEM((ROWS, LANES), F32),
            pltpu.VMEM((ROWS, LANES), F32),
            pltpu.VMEM((NT * LANES, ROWS), BF16),
            pltpu.VMEM((BRICKS, NT * CH, CAP), BF16),
            pltpu.VMEM((BRICKS, NT * CH, CAP), BF16),
            pltpu.VMEM((NT * CH, ATOMS), F32),
            pltpu.VMEM((40, LANES), F32),
            pltpu.VMEM((2, LANES, LANES), BF16),
            pltpu.VMEM((8, LANES), F32),
            dma((3, BRICKS)),
            dma((3, BRICKS)),
            dma((fields, 8)),
            dma((fields, 8)),
            dma((2, BRICKS)),
            dma((2, BRICKS)),
        ],
        compiler_params=pltpu.CompilerParams(
            collective_id=0, has_side_effects=True, vmem_limit_bytes=60 * 1024 * 1024
        ),
    )(
        features, tangents, route.reshape(1, ATOMS), cell_local.reshape(1, ATOMS), stencil.reshape(1, ATOMS),
        stencil_table, taps1, taps2, point1, point2,
        bias1.reshape(1, CH), bias2.reshape(1, CH), readout.reshape(1, CH),
    )
    return picked.reshape(NT, CH, ATOMS).astype(F32) * tab


def solution(mesh):
    placed = (
        P(None, ("slab", "brick")),
        P(None, None, ("slab", "brick")),
        P(("slab", "brick"), None),
        P(("slab", "brick")),
        P(("slab", "brick")),
        P(),
        P(),
        P(),
        P(),
        P(),
        P(),
        P(),
        P(),
    )
    return jax.shard_map(
        shards,
        mesh=mesh,
        in_specs=placed,
        out_specs=P(None, None, ("slab", "brick")),
        check_vma=False,
    )
```

```python
import functools

import jax
import jax.numpy as jnp
from jax import lax
from jax.experimental import pallas as pl
from jax.experimental.pallas import tpu as pltpu
from jax.sharding import PartitionSpec as P

NG = 64
CH = 64
NT = 4
KSETS = 8
BRICKS = 8
SLABS = 16
ATOMS = 2048
CAP = 512
CZ = 4
CY = 8
XH = 32
LANES = 2 * CH
ROWS = CZ * CY * XH
HEAD = 16
GROUPS = ((HEAD, 3 * CH), (HEAD + 3 * CH, 2 * CH), (0, HEAD))
DEPTH = HEAD + (NT + 1) * CH
F32 = jnp.float32
BF16 = jnp.bfloat16
MESH = pl.DeviceIdType.MESH
VMEM = pl.BlockSpec(memory_space=pltpu.VMEM)


def owner(brick):
    side = brick // 4
    return 2 * (brick + side * (7 - 2 * brick)) + side


def twice(value):
    return jnp.concatenate([value, value], axis=-1)


def whole_kernel(*refs):
    sources, (picked, tab), inputs, rest = refs[:13], refs[13:15], refs[15:28], refs[28:]
    (
        feat, tang, route, cell, sten, table, taps_one, taps_two,
        point_one, point_two, bias_one, bias_two, readout,
    ) = inputs
    (
        data, place_in, place_out, column, slots, packed, recv, hot, ext, acc, t_one, slope, bend, curve,
        final, send, got, total, taps, mixers, rows3,
        a_send, a_recv, h_send, h_recv, b_send, b_recv, load_sem,
    ) = rest
    slab = lax.axis_index("slab")
    place = lax.axis_index("brick")
    x_hi = place % 2
    y = place // 2
    brick = y + x_hi * (7 - 2 * y)
    s_up, s_down = (slab + 1) % SLABS, (slab + SLABS - 1) % SLABS
    b_up, b_down = owner((brick + 1) % BRICKS), owner((brick + BRICKS - 1) % BRICKS)

    def at(s, b):
        return {"slab": s, "brick": b}

    peers = [at(slab, (place + r) % BRICKS) for r in range(1, BRICKS)]
    around = [
        at(s_down, place), at(s_up, place),
        at(s_down, b_down), at(s_down, b_up), at(s_up, b_down), at(s_up, b_up),
    ]
    gate = pltpu.get_barrier_semaphore()
    for peer in peers + around:
        pl.semaphore_signal(gate, inc=1, device_id=peer, device_id_type=MESH)
    loads = [
        pltpu.make_async_copy(source, target, load_sem.at[i])
        for i, (source, target) in enumerate(zip(sources, inputs))
    ]
    for load in loads:
        load.start()
    for load in loads:
        load.wait()

    def forward(g, r):
        start, size = GROUPS[g]
        return pltpu.make_async_remote_copy(
            src_ref=packed.at[r, pl.ds(start, size)],
            dst_ref=recv.at[r, pl.ds(start, size)],
            send_sem=a_send.at[g, r],
            recv_sem=a_recv.at[g, r],
            device_id=at(slab, (place + r) % BRICKS),
            device_id_type=MESH,
        )

    def prepare():
        table_t = jnp.transpose(twice(table[...]))
        step = 512
        for c in range(ATOMS // step):
            cols = slice(c * step, (c + 1) * step)
            chosen = jnp.broadcast_to(table_t[0:CH, 0:1], (CH, step))
            for k in range(1, KSETS):
                chosen = jnp.where(sten[:, cols] == k, table_t[0:CH, k : k + 1], chosen)
            tab[:, cols] = chosen
            cells = cell[:, cols]
            high = (cells // NG + 1).astype(F32)
            low = (cells % NG).astype(F32)
            which = lax.broadcasted_iota(jnp.int32, (HEAD, step), 0)
            head = jnp.where(which == 0, high, jnp.where(which == 1, low, 0.0))
            data[0:HEAD, cols] = head.astype(BF16)
            data[HEAD : HEAD + CH, cols] = (feat[:, cols].astype(F32) * chosen).astype(BF16)
            for k in range(NT):
                start = HEAD + (k + 1) * CH
                data[start : start + CH, cols] = (tang[k, :, cols].astype(F32) * chosen).astype(BF16)
        width = 256
        upper = lax.broadcasted_iota(jnp.int32, (width, width), 0) <= lax.broadcasted_iota(
            jnp.int32, (width, width), 1
        )
        upper = jnp.where(upper, 1.0, 0.0).astype(BF16)
        carry = jnp.zeros((BRICKS, 1), F32)
        for c in range(ATOMS // width):
            cols = slice(c * width, (c + 1) * width)
            dest = (owner(route[:, cols]) - place + BRICKS) % BRICKS
            hit = lax.broadcasted_iota(jnp.int32, (BRICKS, width), 0) == dest
            one = jnp.where(hit, 1.0, 0.0)
            count = jnp.dot(one.astype(BF16), upper, preferred_element_type=F32) + carry
            position = jnp.sum(jnp.where(hit, count, 0.0), axis=0, keepdims=True) - 1.0
            slot = jnp.broadcast_to(dest.astype(F32) * CAP + position, (8, width))
            slots[:, cols] = slot
            column[cols, :] = jnp.transpose(slot)
            carry = carry + jnp.sum(one, axis=1, keepdims=True)
        for stage, (source, flip) in enumerate(
            ((taps_one, False), (taps_two, False), (taps_two, True), (taps_one, True))
        ):
            for axis in range(3):
                for tap in range(3):
                    i = stage * 9 + axis * 3 + tap
                    j = 2 - tap if flip else tap
                    taps[i : i + 1, :] = twice(source[axis, j : j + 1, :])
        rows3[0:1, :] = twice(bias_one[...])
        rows3[1:2, :] = twice(bias_two[...])
        rows3[2:3, :] = twice(readout[...])
        for i, point in enumerate((point_one, point_two)):
            value = point[...].astype(F32)
            zero = jnp.zeros_like(value)
            mixers[i, 0:CH, :] = jnp.concatenate([value, zero], axis=1).astype(BF16)
            mixers[i, CH:LANES, :] = jnp.concatenate([zero, value], axis=1).astype(BF16)

    def pack(r):
        base = r * CAP
        for c in range(ATOMS // 128):
            rows = slice(c * 128, (c + 1) * 128)
            lane = (lax.broadcasted_iota(jnp.int32, (128, CAP), 1) + base).astype(F32)
            place_in[rows, :] = jnp.where(column[rows, 0:1] == lane, 1.0, 0.0).astype(BF16)
        return jnp.dot(data[...], place_in[...], preferred_element_type=F32).astype(BF16)

    def unpack(r):
        def block(i, _):
            row = (lax.broadcasted_iota(jnp.int32, (64, ATOMS), 0) + (i * 64 + r * CAP)).astype(F32)
            place_out[pl.ds(pl.multiple_of(i * 64, 64), 64), :] = jnp.where(
                row == slots[0:1, :], 1.0, 0.0
            ).astype(BF16)
            return 0

        lax.fori_loop(0, CAP // 64, block, 0)
        return jnp.dot(got[r], place_out[...], preferred_element_type=F32)

    def halo(stage, v):
        e = stage * (NT + 1) + v
        field = ext.at[e]
        moves = (
            (field.at[1, 1], field.at[CZ + 1, CY + 1], at(s_down, b_down)),
            (field.at[1, CY], field.at[CZ + 1, 0], at(s_down, b_up)),
            (field.at[CZ, 1], field.at[0, CY + 1], at(s_up, b_down)),
            (field.at[CZ, CY], field.at[0, 0], at(s_up, b_up)),
            (field.at[pl.ds(1, CZ), 1], field.at[pl.ds(1, CZ), CY + 1], at(slab, b_down)),
            (field.at[pl.ds(1, CZ), CY], field.at[pl.ds(1, CZ), 0], at(slab, b_up)),
            (field.at[1, pl.ds(1, CY)], field.at[CZ + 1, pl.ds(1, CY)], at(s_down, place)),
            (field.at[CZ, pl.ds(1, CY)], field.at[0, pl.ds(1, CY)], at(s_up, place)),
        )
        return [
            pltpu.make_async_remote_copy(
                src_ref=src,
                dst_ref=dst,
                send_sem=h_send.at[e, i],
                recv_sem=h_recv.at[e, i],
                device_id=to,
                device_id_type=MESH,
            )
            for i, (src, dst, to) in enumerate(moves)
        ]

    def launch(stage, v):
        for copy in halo(stage, v):
            copy.start()

    def arrive(stage, v):
        for copy in halo(stage, v):
            copy.wait_recv()

    def split_mask(r):
        low = recv[r, 0:HEAD, :].astype(F32)[1:2, :]
        return low >= XH

    def make_hot(r):
        head = recv[r, 0:HEAD, :].astype(F32)
        high, low = head[0:1, :], head[1:2, :]
        label = (high - 1.0) * XH + jnp.where(low >= XH, low - XH, low)

        def block(i, _):
            row = (lax.broadcasted_iota(jnp.int32, (128, CAP), 0) + i * 128).astype(F32)
            hot[r, pl.ds(pl.multiple_of(i * 128, 128), 128), :] = jnp.where(
                row == label, 1.0, 0.0
            ).astype(BF16)
            return 0

        lax.fori_loop(0, ROWS // 128, block, 0)

    def deposit(g, low, high):
        vectors, first = (3, 0) if g == 0 else (2, 3)
        width = LANES * vectors

        def source(r, _):
            if low > 0:
                forward(g, r).wait_recv()
            upper = split_mask(r)
            parts = []
            for i in range(vectors):
                rows = HEAD + (first + i) * CH
                value = recv[r, rows : rows + CH, :].astype(F32)
                parts.append(jnp.where(upper, 0.0, value).astype(BF16))
                parts.append(jnp.where(upper, value, 0.0).astype(BF16))
            spread = jnp.concatenate(parts, axis=0)
            more = lax.dot_general(
                hot[r], spread, (((1,), (1,)), ((), ())), preferred_element_type=F32
            )
            if low > 0:
                acc[:, 0:width] += more
            else:
                acc[:, 0:width] = more
            return 0

        if low == 0:
            source(0, 0)
        else:
            lax.fori_loop(low, high, source, 0)
        if high == BRICKS:
            for i in range(vectors):
                for z in range(CZ):
                    part = acc[z * CY * XH : (z + 1) * CY * XH, i * LANES : (i + 1) * LANES]
                    ext[first + i, z + 1, 1 : CY + 1] = part.astype(BF16).reshape(CY, XH, LANES)
                launch(0, first + i)

    def bulk(g, low, high):
        for r in range(low, high):
            forward(g, r).start()

    def convolve(stage, v, z):
        e = stage * (NT + 1) + v

        def weight(axis, tap):
            i = stage * 9 + axis * 3 + tap
            return taps[i : i + 1, :].reshape(1, 1, LANES)

        along = (
            weight(0, 0) * ext[e, z].astype(F32)
            + weight(0, 1) * ext[e, z + 1].astype(F32)
            + weight(0, 2) * ext[e, z + 2].astype(F32)
        )
        across = (
            weight(1, 0) * along[0:CY]
            + weight(1, 1) * along[1 : CY + 1]
            + weight(1, 2) * along[2 : CY + 2]
        )
        flat = across.reshape(CY, XH, LANES)
        sub = lax.broadcasted_iota(jnp.int32, (CY, 8, LANES), 1)
        back_one = pltpu.roll(flat, 1, 1)
        first = back_one[:, 0:8, :]
        first = jnp.where(sub == 0, pltpu.roll(first, CH, 2), first)
        before = jnp.concatenate([first, back_one[:, 8:, :]], axis=1)
        on_one = pltpu.roll(flat, XH - 1, 1)
        last = on_one[:, XH - 8 :, :]
        last = jnp.where(sub == 7, pltpu.roll(last, CH, 2), last)
        after = jnp.concatenate([on_one[:, : XH - 8, :], last], axis=1)
        out = weight(2, 0) * before + weight(2, 1) * flat + weight(2, 2) * after
        return out.reshape(CY * XH, LANES)

    plane = CY * XH

    def span(z):
        return slice(z * plane, (z + 1) * plane)

    def mix(value, i, back):
        sides = ((1,), (0,)) if back else ((1,), (1,))
        return lax.dot_general(
            value.astype(BF16), mixers[i], (sides, ((), ())), preferred_element_type=F32
        )

    def put(stage, v, z, value):
        ext[stage * (NT + 1) + v, z + 1, 1 : CY + 1] = value.astype(BF16).reshape(CY, XH, LANES)

    def planes(body):
        for z in range(CZ):
            body(z)

    def sweep(stage, body, low, high):
        def step(v, _):
            arrive(stage, v)
            planes(functools.partial(body, v))
            if stage < 3:
                launch(stage + 1, v)
            return 0

        lax.fori_loop(low, high, step, 0)

    def base_one(v, z):
        pre = mix(convolve(0, 0, z), 0, False) + rows3[0:1, :]
        sg = jax.nn.sigmoid(pre)
        slope[span(z), :] = sg * (1.0 + pre * (1.0 - sg))
        bend[span(z), :] = sg * (1.0 - sg) * (2.0 + pre * (1.0 - 2.0 * sg))
        put(1, 0, z, pre * sg)

    def tangent_one(v, z):
        t = mix(convolve(0, v, z), 0, False)
        t_one[v - 1, span(z), :] = t
        put(1, v, z, slope[span(z), :] * t)

    def base_two(v, z):
        pre = mix(convolve(1, 0, z), 1, False) + rows3[1:2, :]
        sg = jax.nn.sigmoid(pre)
        scale = rows3[2:3, :]
        curve[span(z), :] = sg * (1.0 - sg) * (2.0 + pre * (1.0 - 2.0 * sg)) * scale
        put(2, 0, z, mix(sg * (1.0 + pre * (1.0 - sg)) * scale, 1, True))

    def tangent_two(v, z):
        dz = mix(convolve(1, v, z), 1, False)
        put(2, v, z, mix(curve[span(z), :] * dz, 1, True))

    def base_three(z):
        bend[span(z), :] = bend[span(z), :] * convolve(2, 0, z)

    def tangent_three(v, z):
        term = bend[span(z), :] * t_one[v - 1, span(z), :] + slope[span(z), :] * convolve(2, v, z)
        put(3, v, z, mix(term, 0, True))

    def tangent_four(v, z):
        out = jnp.transpose(convolve(3, v, z)).astype(BF16)
        final[pl.ds(pl.multiple_of((v - 1) * LANES, LANES), LANES), span(z)] = out

    def backward(p, r):
        return pltpu.make_async_remote_copy(
            src_ref=send.at[r, pl.ds(p * LANES, LANES)],
            dst_ref=got.at[r, pl.ds(p * LANES, LANES)],
            send_sem=b_send.at[p, r],
            recv_sem=b_recv.at[p, r],
            device_id=at(slab, (place + BRICKS - r) % BRICKS),
            device_id_type=MESH,
        )

    def pick(p, low, high):
        def source(r, _):
            fetched = jnp.dot(
                final[2 * p * LANES : 2 * (p + 1) * LANES, :], hot[r], preferred_element_type=F32
            )
            upper = split_mask(r)
            parts = []
            for k in range(2):
                at_k = k * LANES
                parts.append(
                    jnp.where(upper, fetched[at_k + CH : at_k + LANES], fetched[at_k : at_k + CH])
                )
            chosen = jnp.concatenate(parts, axis=0).astype(BF16)

            @pl.when(r > 0)
            def _():
                send[r, p * LANES : (p + 1) * LANES, :] = chosen
                backward(p, r).start()

            @pl.when(r == 0)
            def _():
                got[0, p * LANES : (p + 1) * LANES, :] = chosen

            return 0

        lax.fori_loop(low, high, source, 0)

    def collect(r, _):
        for p in range(2):
            backward(p, r).wait_recv()
        total[...] += unpack(r)
        return 0

    prepare()
    recv[0] = pack(0)

    def pack_only(r, _):
        packed[r] = pack(r)
        return 0

    def pack_and_send(r, _):
        packed[r] = pack(r)
        forward(2, r).start()
        forward(0, r).start()
        return 0

    early = 2
    lax.fori_loop(1, early, pack_only, 0)
    pl.semaphore_wait(gate, len(peers) + len(around))
    for r in range(1, early):
        forward(2, r).start()
        forward(0, r).start()
    lax.fori_loop(early, BRICKS, pack_and_send, 0)
    bulk(1, 1, BRICKS)
    make_hot(0)
    deposit(0, 0, 1)

    def mark(r, _):
        forward(2, r).wait_recv()
        make_hot(r)
        return 0

    lax.fori_loop(1, BRICKS, mark, 0)
    deposit(0, 1, 8)
    sweep(0, base_one, 0, 1)
    sweep(0, tangent_one, 1, 3)
    deposit(1, 0, 1)
    deposit(1, 1, 8)
    sweep(1, base_two, 0, 1)
    sweep(1, tangent_two, 1, 3)
    sweep(0, tangent_one, 3, 5)
    arrive(2, 0)
    planes(base_three)
    sweep(2, tangent_three, 1, 3)
    sweep(1, tangent_two, 3, 5)
    sweep(3, tangent_four, 1, 3)
    sweep(2, tangent_three, 3, 5)
    pick(0, 0, 8)
    sweep(3, tangent_four, 3, 5)
    pick(1, 0, 8)
    total[...] = unpack(0)
    lax.fori_loop(1, BRICKS, collect, 0)
    picked[...] = total[...].astype(BF16)

    def finish(r, _):
        for p in range(2):
            backward(p, r).wait_send()
        for g in range(len(GROUPS)):
            forward(g, r).wait_send()
        return 0

    lax.fori_loop(1, BRICKS, finish, 0)

    def finish_halo(v, _):
        for stage in range(4):
            if stage == 3:
                @pl.when(v > 0)
                def _():
                    for copy in halo(3, v):
                        copy.wait_send()
            else:
                for copy in halo(stage, v):
                    copy.wait_send()
        return 0

    lax.fori_loop(0, NT + 1, finish_halo, 0)


def shards(
    features, tangents, route, cell_local, stencil, stencil_table,
    taps1, taps2, point1, point2, bias1, bias2, readout,
):
    fields = 4 * (NT + 1)
    dma = pltpu.SemaphoreType.DMA
    operands = (
        features, tangents, route.reshape(1, ATOMS), cell_local.reshape(1, ATOMS), stencil.reshape(1, ATOMS),
        stencil_table, taps1, taps2, point1, point2,
        bias1.reshape(1, CH), bias2.reshape(1, CH), readout.reshape(1, CH),
    )
    picked, tab = pl.pallas_call(
        whole_kernel,
        name="whole",
        out_shape=(
            jax.ShapeDtypeStruct((NT * CH, ATOMS), BF16),
            jax.ShapeDtypeStruct((CH, ATOMS), F32),
        ),
        in_specs=[pl.BlockSpec(memory_space=pltpu.HBM)] * 13,
        out_specs=(VMEM, VMEM),
        scratch_shapes=[pltpu.VMEM(value.shape, value.dtype) for value in operands]
        + [
            pltpu.VMEM((DEPTH, ATOMS), BF16),
            pltpu.VMEM((ATOMS, CAP), BF16),
            pltpu.VMEM((CAP, ATOMS), BF16),
            pltpu.VMEM((ATOMS, 8), F32),
            pltpu.VMEM((8, ATOMS), F32),
            pltpu.VMEM((BRICKS, DEPTH, CAP), BF16),
            pltpu.VMEM((BRICKS, DEPTH, CAP), BF16),
            pltpu.VMEM((BRICKS, ROWS, CAP), BF16),
            pltpu.VMEM((fields, CZ + 2, CY + 2, XH, LANES), BF16),
            pltpu.VMEM((ROWS, 3 * LANES), F32),
            pltpu.VMEM((NT, ROWS, LANES), F32),
            pltpu.VMEM((ROWS, LANES), F32),
            pltpu.VMEM((ROWS, LANES), F32),
            pltpu.VMEM((ROWS, LANES), F32),
            pltpu.VMEM((NT * LANES, ROWS), BF16),
            pltpu.VMEM((BRICKS, NT * CH, CAP), BF16),
            pltpu.VMEM((BRICKS, NT * CH, CAP), BF16),
            pltpu.VMEM((NT * CH, ATOMS), F32),
            pltpu.VMEM((40, LANES), F32),
            pltpu.VMEM((2, LANES, LANES), BF16),
            pltpu.VMEM((8, LANES), F32),
            dma((3, BRICKS)),
            dma((3, BRICKS)),
            dma((fields, 8)),
            dma((fields, 8)),
            dma((2, BRICKS)),
            dma((2, BRICKS)),
            dma((13,)),
        ],
        compiler_params=pltpu.CompilerParams(
            collective_id=0, has_side_effects=True, vmem_limit_bytes=50 * 1024 * 1024
        ),
    )(*(pltpu.with_memory_space_constraint(value, pltpu.HBM) for value in operands))
    return picked.reshape(NT, CH, ATOMS).astype(F32) * tab


def solution(mesh):
    placed = (
        P(None, ("slab", "brick")),
        P(None, None, ("slab", "brick")),
        P(("slab", "brick"), None),
        P(("slab", "brick")),
        P(("slab", "brick")),
        P(),
        P(),
        P(),
        P(),
        P(),
        P(),
        P(),
        P(),
    )
    return jax.shard_map(
        shards,
        mesh=mesh,
        in_specs=placed,
        out_specs=P(None, None, ("slab", "brick")),
        check_vma=False,
    )
```

```python
import functools

import jax
import jax.numpy as jnp
from jax import lax
from jax.experimental import pallas as pl
from jax.experimental.pallas import tpu as pltpu
from jax.sharding import PartitionSpec as P

NG = 64
CH = 64
NT = 4
KSETS = 8
BRICKS = 8
SLABS = 16
ATOMS = 2048
CAP = 512
CZ = 4
CY = 8
XH = 32
LANES = 2 * CH
ROWS = CZ * CY * XH
HEAD = 16
GROUPS = ((HEAD, 3 * CH), (HEAD + 3 * CH, 2 * CH), (0, HEAD))
DEPTH = HEAD + (NT + 1) * CH
F32 = jnp.float32
BF16 = jnp.bfloat16
MESH = pl.DeviceIdType.MESH
VMEM = pl.BlockSpec(memory_space=pltpu.VMEM)


def owner(brick):
    side = brick // 4
    return 2 * (brick + side * (7 - 2 * brick)) + side


def twice(value):
    return jnp.concatenate([value, value], axis=-1)


def whole_kernel(*refs):
    sources, (picked, tab), inputs, rest = refs[:13], refs[13:15], refs[15:28], refs[28:]
    (
        feat, tang, route, cell, sten, table, taps_one, taps_two,
        point_one, point_two, bias_one, bias_two, readout,
    ) = inputs
    (
        data, place_in, place_out, column, slots, packed, recv, hot, ext, acc, t_one, slope, bend, curve,
        final, send, got, total, taps, mixers, rows3,
        a_send, a_recv, h_send, h_recv, b_send, b_recv, load_sem,
    ) = rest
    slab = lax.axis_index("slab")
    place = lax.axis_index("brick")
    x_hi = place % 2
    y = place // 2
    brick = y + x_hi * (7 - 2 * y)
    s_up, s_down = (slab + 1) % SLABS, (slab + SLABS - 1) % SLABS
    b_up, b_down = owner((brick + 1) % BRICKS), owner((brick + BRICKS - 1) % BRICKS)

    def at(s, b):
        return {"slab": s, "brick": b}

    peers = [at(slab, (place + r) % BRICKS) for r in range(1, BRICKS)]
    around = [
        at(s_down, place), at(s_up, place),
        at(s_down, b_down), at(s_down, b_up), at(s_up, b_down), at(s_up, b_up),
    ]
    gate = pltpu.get_barrier_semaphore()
    for peer in peers + around:
        pl.semaphore_signal(gate, inc=1, device_id=peer, device_id_type=MESH)
    loads = [
        pltpu.make_async_copy(source, target, load_sem.at[i])
        for i, (source, target) in enumerate(zip(sources, inputs))
    ]
    for load in loads:
        load.start()
    for load in loads:
        load.wait()

    def forward(g, r):
        start, size = GROUPS[g]
        return pltpu.make_async_remote_copy(
            src_ref=packed.at[r, pl.ds(start, size)],
            dst_ref=recv.at[r, pl.ds(start, size)],
            send_sem=a_send.at[g, r],
            recv_sem=a_recv.at[g, r],
            device_id=at(slab, (place + r) % BRICKS),
            device_id_type=MESH,
        )

    def prepare():
        table_t = jnp.transpose(twice(table[...]))
        step = 512
        for c in range(ATOMS // step):
            cols = slice(c * step, (c + 1) * step)
            chosen = jnp.broadcast_to(table_t[0:CH, 0:1], (CH, step))
            for k in range(1, KSETS):
                chosen = jnp.where(sten[:, cols] == k, table_t[0:CH, k : k + 1], chosen)
            tab[:, cols] = chosen
            cells = cell[:, cols]
            high = (cells // NG + 1).astype(F32)
            low = (cells % NG).astype(F32)
            which = lax.broadcasted_iota(jnp.int32, (HEAD, step), 0)
            head = jnp.where(which == 0, high, jnp.where(which == 1, low, 0.0))
            data[0:HEAD, cols] = head.astype(BF16)
            data[HEAD : HEAD + CH, cols] = (feat[:, cols].astype(F32) * chosen).astype(BF16)
            for k in range(NT):
                start = HEAD + (k + 1) * CH
                data[start : start + CH, cols] = (tang[k, :, cols].astype(F32) * chosen).astype(BF16)
        width = 256
        upper = lax.broadcasted_iota(jnp.int32, (width, width), 0) <= lax.broadcasted_iota(
            jnp.int32, (width, width), 1
        )
        upper = jnp.where(upper, 1.0, 0.0).astype(BF16)
        carry = jnp.zeros((BRICKS, 1), F32)
        for c in range(ATOMS // width):
            cols = slice(c * width, (c + 1) * width)
            dest = (owner(route[:, cols]) - place + BRICKS) % BRICKS
            hit = lax.broadcasted_iota(jnp.int32, (BRICKS, width), 0) == dest
            one = jnp.where(hit, 1.0, 0.0)
            count = jnp.dot(one.astype(BF16), upper, preferred_element_type=F32) + carry
            position = jnp.sum(jnp.where(hit, count, 0.0), axis=0, keepdims=True) - 1.0
            slot = jnp.broadcast_to(dest.astype(F32) * CAP + position, (8, width))
            slots[:, cols] = slot
            column[cols, :] = jnp.transpose(slot)
            carry = carry + jnp.sum(one, axis=1, keepdims=True)
        for stage, (source, flip) in enumerate(
            ((taps_one, False), (taps_two, False), (taps_two, True), (taps_one, True))
        ):
            for axis in range(3):
                for tap in range(3):
                    i = stage * 9 + axis * 3 + tap
                    j = 2 - tap if flip else tap
                    taps[i : i + 1, :] = twice(source[axis, j : j + 1, :])
        rows3[0:1, :] = twice(bias_one[...])
        rows3[1:2, :] = twice(bias_two[...])
        rows3[2:3, :] = twice(readout[...])
        for i, point in enumerate((point_one, point_two)):
            value = point[...].astype(F32)
            zero = jnp.zeros_like(value)
            mixers[i, 0:CH, :] = jnp.concatenate([value, zero], axis=1).astype(BF16)
            mixers[i, CH:LANES, :] = jnp.concatenate([zero, value], axis=1).astype(BF16)

    def pack(r):
        base = r * CAP
        for c in range(ATOMS // 128):
            rows = slice(c * 128, (c + 1) * 128)
            lane = (lax.broadcasted_iota(jnp.int32, (128, CAP), 1) + base).astype(F32)
            place_in[rows, :] = jnp.where(column[rows, 0:1] == lane, 1.0, 0.0).astype(BF16)
        return jnp.dot(data[...], place_in[...], preferred_element_type=F32).astype(BF16)

    def unpack(r):
        def block(i, _):
            row = (lax.broadcasted_iota(jnp.int32, (64, ATOMS), 0) + (i * 64 + r * CAP)).astype(F32)
            place_out[pl.ds(pl.multiple_of(i * 64, 64), 64), :] = jnp.where(
                row == slots[0:1, :], 1.0, 0.0
            ).astype(BF16)
            return 0

        lax.fori_loop(0, CAP // 64, block, 0)
        return jnp.dot(got[r], place_out[...], preferred_element_type=F32)

    def halo(stage, v):
        e = stage * (NT + 1) + v
        field = ext.at[e]
        moves = (
            (field.at[1, 1], field.at[CZ + 1, CY + 1], at(s_down, b_down)),
            (field.at[1, CY], field.at[CZ + 1, 0], at(s_down, b_up)),
            (field.at[CZ, 1], field.at[0, CY + 1], at(s_up, b_down)),
            (field.at[CZ, CY], field.at[0, 0], at(s_up, b_up)),
            (field.at[pl.ds(1, CZ), 1], field.at[pl.ds(1, CZ), CY + 1], at(slab, b_down)),
            (field.at[pl.ds(1, CZ), CY], field.at[pl.ds(1, CZ), 0], at(slab, b_up)),
            (field.at[1, pl.ds(1, CY)], field.at[CZ + 1, pl.ds(1, CY)], at(s_down, place)),
            (field.at[CZ, pl.ds(1, CY)], field.at[0, pl.ds(1, CY)], at(s_up, place)),
        )
        return [
            pltpu.make_async_remote_copy(
                src_ref=src,
                dst_ref=dst,
                send_sem=h_send.at[e, i],
                recv_sem=h_recv.at[e, i],
                device_id=to,
                device_id_type=MESH,
            )
            for i, (src, dst, to) in enumerate(moves)
        ]

    def launch(stage, v):
        for copy in halo(stage, v):
            copy.start()

    def arrive(stage, v, which):
        copies = halo(stage, v)
        for i in which:
            copies[i].wait_recv()

    def split_mask(r):
        low = recv[r, 0:HEAD, :].astype(F32)[1:2, :]
        return low >= XH

    def make_hot(r):
        head = recv[r, 0:HEAD, :].astype(F32)
        high, low = head[0:1, :], head[1:2, :]
        label = (high - 1.0) * XH + jnp.where(low >= XH, low - XH, low)

        def block(i, _):
            row = (lax.broadcasted_iota(jnp.int32, (128, CAP), 0) + i * 128).astype(F32)
            hot[r, pl.ds(pl.multiple_of(i * 128, 128), 128), :] = jnp.where(
                row == label, 1.0, 0.0
            ).astype(BF16)
            return 0

        lax.fori_loop(0, ROWS // 128, block, 0)

    def deposit(g, low, high):
        vectors, first = (3, 0) if g == 0 else (2, 3)
        width = LANES * vectors

        def source(r, _):
            if low > 0:
                forward(g, r).wait_recv()
            upper = split_mask(r)
            parts = []
            for i in range(vectors):
                rows = HEAD + (first + i) * CH
                value = recv[r, rows : rows + CH, :].astype(F32)
                parts.append(jnp.where(upper, 0.0, value).astype(BF16))
                parts.append(jnp.where(upper, value, 0.0).astype(BF16))
            spread = jnp.concatenate(parts, axis=0)
            more = lax.dot_general(
                hot[r], spread, (((1,), (1,)), ((), ())), preferred_element_type=F32
            )
            if low > 0:
                acc[:, 0:width] += more
            else:
                acc[:, 0:width] = more
            return 0

        if low == 0:
            source(0, 0)
        else:
            lax.fori_loop(low, high, source, 0)
        if high == BRICKS:
            for i in range(vectors):
                for z in range(CZ):
                    part = acc[z * CY * XH : (z + 1) * CY * XH, i * LANES : (i + 1) * LANES]
                    ext[first + i, z + 1, 1 : CY + 1] = part.astype(BF16).reshape(CY, XH, LANES)
                launch(0, first + i)

    def bulk(g, low, high):
        for r in range(low, high):
            forward(g, r).start()

    def convolve(stage, v, z):
        e = stage * (NT + 1) + v

        def weight(axis, tap):
            i = stage * 9 + axis * 3 + tap
            return taps[i : i + 1, :].reshape(1, 1, LANES)

        along = (
            weight(0, 0) * ext[e, z].astype(F32)
            + weight(0, 1) * ext[e, z + 1].astype(F32)
            + weight(0, 2) * ext[e, z + 2].astype(F32)
        )
        across = (
            weight(1, 0) * along[0:CY]
            + weight(1, 1) * along[1 : CY + 1]
            + weight(1, 2) * along[2 : CY + 2]
        )
        flat = across.reshape(CY, XH, LANES)
        sub = lax.broadcasted_iota(jnp.int32, (CY, 8, LANES), 1)
        back_one = pltpu.roll(flat, 1, 1)
        first = back_one[:, 0:8, :]
        first = jnp.where(sub == 0, pltpu.roll(first, CH, 2), first)
        before = jnp.concatenate([first, back_one[:, 8:, :]], axis=1)
        on_one = pltpu.roll(flat, XH - 1, 1)
        last = on_one[:, XH - 8 :, :]
        last = jnp.where(sub == 7, pltpu.roll(last, CH, 2), last)
        after = jnp.concatenate([on_one[:, : XH - 8, :], last], axis=1)
        out = weight(2, 0) * before + weight(2, 1) * flat + weight(2, 2) * after
        return out.reshape(CY * XH, LANES)

    plane = CY * XH

    def span(z):
        return slice(z * plane, (z + 1) * plane)

    def mix(value, i, back):
        sides = ((1,), (0,)) if back else ((1,), (1,))
        return lax.dot_general(
            value.astype(BF16), mixers[i], (sides, ((), ())), preferred_element_type=F32
        )

    def put(stage, v, z, value):
        ext[stage * (NT + 1) + v, z + 1, 1 : CY + 1] = value.astype(BF16).reshape(CY, XH, LANES)

    def planes(stage, v, body):
        arrive(stage, v, (4, 5))
        for z in range(1, CZ - 1):
            body(z)
        arrive(stage, v, (0, 1, 2, 3, 6, 7))
        body(0)
        body(CZ - 1)

    def sweep(stage, body, low, high):
        def step(v, _):
            planes(stage, v, functools.partial(body, v))
            if stage < 3:
                launch(stage + 1, v)
            return 0

        lax.fori_loop(low, high, step, 0)

    def base_one(v, z):
        pre = mix(convolve(0, 0, z), 0, False) + rows3[0:1, :]
        sg = jax.nn.sigmoid(pre)
        slope[span(z), :] = sg * (1.0 + pre * (1.0 - sg))
        bend[span(z), :] = sg * (1.0 - sg) * (2.0 + pre * (1.0 - 2.0 * sg))
        put(1, 0, z, pre * sg)

    def tangent_one(v, z):
        t = mix(convolve(0, v, z), 0, False)
        t_one[v - 1, span(z), :] = t
        put(1, v, z, slope[span(z), :] * t)

    def base_two(v, z):
        pre = mix(convolve(1, 0, z), 1, False) + rows3[1:2, :]
        sg = jax.nn.sigmoid(pre)
        scale = rows3[2:3, :]
        curve[span(z), :] = sg * (1.0 - sg) * (2.0 + pre * (1.0 - 2.0 * sg)) * scale
        put(2, 0, z, mix(sg * (1.0 + pre * (1.0 - sg)) * scale, 1, True))

    def tangent_two(v, z):
        dz = mix(convolve(1, v, z), 1, False)
        put(2, v, z, mix(curve[span(z), :] * dz, 1, True))

    def base_three(z):
        bend[span(z), :] = bend[span(z), :] * convolve(2, 0, z)

    def tangent_three(v, z):
        term = bend[span(z), :] * t_one[v - 1, span(z), :] + slope[span(z), :] * convolve(2, v, z)
        put(3, v, z, mix(term, 0, True))

    def tangent_four(v, z):
        out = jnp.transpose(convolve(3, v, z)).astype(BF16)
        final[pl.ds(pl.multiple_of((v - 1) * LANES, LANES), LANES), span(z)] = out

    def backward(p, r):
        return pltpu.make_async_remote_copy(
            src_ref=send.at[r, pl.ds(p * LANES, LANES)],
            dst_ref=got.at[r, pl.ds(p * LANES, LANES)],
            send_sem=b_send.at[p, r],
            recv_sem=b_recv.at[p, r],
            device_id=at(slab, (place + BRICKS - r) % BRICKS),
            device_id_type=MESH,
        )

    def pick(p, low, high):
        def source(r, _):
            fetched = jnp.dot(
                final[2 * p * LANES : 2 * (p + 1) * LANES, :], hot[r], preferred_element_type=F32
            )
            upper = split_mask(r)
            parts = []
            for k in range(2):
                at_k = k * LANES
                parts.append(
                    jnp.where(upper, fetched[at_k + CH : at_k + LANES], fetched[at_k : at_k + CH])
                )
            chosen = jnp.concatenate(parts, axis=0).astype(BF16)

            @pl.when(r > 0)
            def _():
                send[r, p * LANES : (p + 1) * LANES, :] = chosen
                backward(p, r).start()

            @pl.when(r == 0)
            def _():
                got[0, p * LANES : (p + 1) * LANES, :] = chosen

            return 0

        lax.fori_loop(low, high, source, 0)

    def collect(r, _):
        for p in range(2):
            backward(p, r).wait_recv()
        total[...] += unpack(r)
        return 0

    prepare()
    recv[0] = pack(0)

    def pack_only(r, _):
        packed[r] = pack(r)
        return 0

    def pack_and_send(r, _):
        packed[r] = pack(r)
        forward(2, r).start()
        forward(0, r).start()
        return 0

    early = 2
    lax.fori_loop(1, early, pack_only, 0)
    pl.semaphore_wait(gate, len(peers) + len(around))
    for r in range(1, early):
        forward(2, r).start()
        forward(0, r).start()
    lax.fori_loop(early, BRICKS, pack_and_send, 0)
    bulk(1, 1, BRICKS)
    make_hot(0)
    deposit(0, 0, 1)

    def mark(r, _):
        forward(2, r).wait_recv()
        make_hot(r)
        return 0

    lax.fori_loop(1, BRICKS, mark, 0)
    deposit(0, 1, 8)
    deposit(1, 0, 1)
    deposit(1, 1, 5)
    sweep(0, base_one, 0, 1)
    sweep(0, tangent_one, 1, 3)
    deposit(1, 5, 8)
    sweep(1, base_two, 0, 1)
    sweep(1, tangent_two, 1, 3)
    sweep(0, tangent_one, 3, 5)
    planes(2, 0, base_three)
    sweep(2, tangent_three, 1, 3)
    sweep(1, tangent_two, 3, 5)
    sweep(3, tangent_four, 1, 3)
    sweep(2, tangent_three, 3, 5)
    pick(0, 0, 8)
    sweep(3, tangent_four, 3, 5)
    pick(1, 0, 8)
    total[...] = unpack(0)
    lax.fori_loop(1, BRICKS, collect, 0)
    picked[...] = total[...].astype(BF16)

    def finish(r, _):
        for p in range(2):
            backward(p, r).wait_send()
        for g in range(len(GROUPS)):
            forward(g, r).wait_send()
        return 0

    lax.fori_loop(1, BRICKS, finish, 0)

    def finish_halo(v, _):
        for stage in range(4):
            if stage == 3:
                @pl.when(v > 0)
                def _():
                    for copy in halo(3, v):
                        copy.wait_send()
            else:
                for copy in halo(stage, v):
                    copy.wait_send()
        return 0

    lax.fori_loop(0, NT + 1, finish_halo, 0)


def shards(
    features, tangents, route, cell_local, stencil, stencil_table,
    taps1, taps2, point1, point2, bias1, bias2, readout,
):
    fields = 4 * (NT + 1)
    dma = pltpu.SemaphoreType.DMA
    operands = (
        features, tangents, route.reshape(1, ATOMS), cell_local.reshape(1, ATOMS), stencil.reshape(1, ATOMS),
        stencil_table, taps1, taps2, point1, point2,
        bias1.reshape(1, CH), bias2.reshape(1, CH), readout.reshape(1, CH),
    )
    picked, tab = pl.pallas_call(
        whole_kernel,
        name="whole",
        out_shape=(
            jax.ShapeDtypeStruct((NT * CH, ATOMS), BF16),
            jax.ShapeDtypeStruct((CH, ATOMS), F32),
        ),
        in_specs=[pl.BlockSpec(memory_space=pltpu.HBM)] * 13,
        out_specs=(VMEM, VMEM),
        scratch_shapes=[pltpu.VMEM(value.shape, value.dtype) for value in operands]
        + [
            pltpu.VMEM((DEPTH, ATOMS), BF16),
            pltpu.VMEM((ATOMS, CAP), BF16),
            pltpu.VMEM((CAP, ATOMS), BF16),
            pltpu.VMEM((ATOMS, 8), F32),
            pltpu.VMEM((8, ATOMS), F32),
            pltpu.VMEM((BRICKS, DEPTH, CAP), BF16),
            pltpu.VMEM((BRICKS, DEPTH, CAP), BF16),
            pltpu.VMEM((BRICKS, ROWS, CAP), BF16),
            pltpu.VMEM((fields, CZ + 2, CY + 2, XH, LANES), BF16),
            pltpu.VMEM((ROWS, 3 * LANES), F32),
            pltpu.VMEM((NT, ROWS, LANES), F32),
            pltpu.VMEM((ROWS, LANES), F32),
            pltpu.VMEM((ROWS, LANES), F32),
            pltpu.VMEM((ROWS, LANES), F32),
            pltpu.VMEM((NT * LANES, ROWS), BF16),
            pltpu.VMEM((BRICKS, NT * CH, CAP), BF16),
            pltpu.VMEM((BRICKS, NT * CH, CAP), BF16),
            pltpu.VMEM((NT * CH, ATOMS), F32),
            pltpu.VMEM((40, LANES), F32),
            pltpu.VMEM((2, LANES, LANES), BF16),
            pltpu.VMEM((8, LANES), F32),
            dma((3, BRICKS)),
            dma((3, BRICKS)),
            dma((fields, 8)),
            dma((fields, 8)),
            dma((2, BRICKS)),
            dma((2, BRICKS)),
            dma((13,)),
        ],
        compiler_params=pltpu.CompilerParams(
            collective_id=0, has_side_effects=True, vmem_limit_bytes=50 * 1024 * 1024
        ),
    )(*(pltpu.with_memory_space_constraint(value, pltpu.HBM) for value in operands))
    return picked.reshape(NT, CH, ATOMS).astype(F32) * tab


def solution(mesh):
    placed = (
        P(None, ("slab", "brick")),
        P(None, None, ("slab", "brick")),
        P(("slab", "brick"), None),
        P(("slab", "brick")),
        P(("slab", "brick")),
        P(),
        P(),
        P(),
        P(),
        P(),
        P(),
        P(),
        P(),
    )
    return jax.shard_map(
        shards,
        mesh=mesh,
        in_specs=placed,
        out_specs=P(None, None, ("slab", "brick")),
        check_vma=False,
    )
```
